512 devices in a mesh: fsdp: 32 (over z, y_hi), tensor: 16 (over x, y_lo, core).
Axes of the slice: x: 4, y: 8 (y_hi: 4, y_lo: 2; y = y_hi * 2 + y_lo), z: 8, core: 2. Of those that a mesh axis runs over, the one named last changes fastest.
Arguments:
- old_codes: bfloat16 [26624, 16384], P(('fsdp', 'tensor')), may hold values from -1 to 1
- old_scales: float32 [208, 128], replicated, may hold values from 0.003 to 0.03
- gate_pre: bfloat16 [2048, 26624], P('fsdp', 'tensor'), may hold values from -6 to 6
- up_pre: bfloat16 [2048, 26624], P('fsdp', 'tensor'), may hold values from -6 to 6
Outputs:
- mixed: bfloat16 [2048, 16384], P('tensor', 'fsdp')
- codes_t: bfloat16 [16384, 26624], P('fsdp', 'tensor')
- scales_t: float32 [128, 208], P('fsdp', 'tensor')
The draws below stay inside these ranges and needn't reach their ends.
All inputs are finite; a program needn't handle non-finite values. Where the reference program divides by a largest or mean magnitude, that divisor is 1e-20 or more.
Results may differ from the reference program's by a relative error of at most 0.024.
Values may be sent and summed in bfloat16 or wider, within the bound.
No kernel may reach another device: no remote copies, remote signals or barrier semaphores. Data moves between devices by JAX's collectives and lax.ppermute only.
A program may use at most 64 MiB of HBM per device.

```python
import math
import jax
import jax.numpy as jnp
from jax import lax

D = 16384
FFW = 26624
TILE = 128
TOKENS = 2048


def block_scale(rng, shape, shards, low, top_value):
    gain, own = 1.0, jax.random.fold_in(rng, 6)
    for axis_at, blocks in shards:
        steps = jnp.exp(jax.random.uniform(jax.random.fold_in(own, axis_at), (blocks,), jnp.float32, low / len(shards), top_value / len(shards)))
        gain = gain * jnp.repeat(steps, shape[axis_at] // blocks).reshape([-1 if axis == axis_at else 1 for axis in range(len(shape))])
    return gain


def normal_values(key, shape, spread, reach, cuts=(), kind=jnp.bfloat16):
    level = block_scale(key, shape, cuts, -0.22, 0.18) if cuts else 1.0
    array = jax.random.normal(key, shape, jnp.float32) * spread * level
    return jnp.minimum(jnp.maximum(array, -reach), reach).astype(kind)


def setup_inputs(seed: int = 0) -> dict:
    key_list = jax.random.split(jax.random.key(seed), 5)
    old_codes = jnp.clip(jax.random.uniform(key_list[0], (FFW, D), jnp.float32, -1.0, 1.0) * block_scale(key_list[0], (FFW, D), ((0, 512),), -0.4, 0.0), -1.0, 1.0).astype(jnp.bfloat16)
    old_scales = jnp.clip(jnp.exp(jax.random.uniform(key_list[1], (FFW // TILE, D // TILE), jnp.float32, math.log(0.003), math.log(0.03))), 0.003, 0.03)
    gate_pre = normal_values(key_list[2], (TOKENS, FFW), 1.0, 6.0, ((0, 32), (1, 16)))
    up_pre = normal_values(key_list[3], (TOKENS, FFW), 1.0, 6.0, ((0, 32), (1, 16)))
    return dict(old_codes=old_codes, old_scales=old_scales, gate_pre=gate_pre, up_pre=up_pre)


epsilon = 1e-6


def reference(old_codes, old_scales, gate_pre, up_pre):
    hidden = (jax.nn.silu(gate_pre.astype(jnp.float32)) * up_pre.astype(jnp.float32)).astype(jnp.bfloat16)
    col_tiles = D // TILE

    def one_tile(running, tile_row):
        first_row = (tile_row * TILE).astype(jnp.int32)
        code_block = lax.dynamic_slice_in_dim(old_codes, first_row, TILE, 0).astype(jnp.float32)
        scale_row = lax.dynamic_slice_in_dim(old_scales, tile_row, 1, 0)
        tile_values = code_block.reshape(TILE, col_tiles, TILE) * scale_row.reshape(1, col_tiles, 1)
        new_scale = jnp.max(jnp.abs(tile_values), axis=(0, 2)) + epsilon
        new_codes = (tile_values / new_scale[None, :, None]).astype(jnp.bfloat16)
        weight = (new_codes.astype(jnp.float32) * new_scale[None, :, None]).astype(jnp.bfloat16).reshape(TILE, D)
        hidden_part = lax.dynamic_slice_in_dim(hidden, first_row, TILE, 1)
        running = running + jnp.dot(hidden_part.astype(jnp.float32), weight.astype(jnp.float32), precision=lax.Precision.HIGHEST)
        return running, (new_codes.reshape(TILE, D), new_scale)

    zero_sum = jnp.zeros((TOKENS, D), jnp.float32)
    running, (new_codes, new_scales) = lax.scan(one_tile, zero_sum, jnp.arange(FFW // TILE, dtype=jnp.int32))
    return running.astype(jnp.bfloat16), new_codes.reshape(FFW, D).T, new_scales.T
```

```python
import jax
import jax.numpy as jnp
from jax import lax
from jax.sharding import Mesh, PartitionSpec as P

TILE = 128
EPSILON = 1e-06
AXES = ("z", "h", "x", "l", "c")
SIZES = (8, 4, 4, 2, 2)
FSDP = ("z", "h")
TENSOR = ("x", "l", "c")


def body(old_codes, old_scales, gate_pre, up_pre):
    n_fsdp = lax.axis_size(FSDP)
    n_tensor = lax.axis_size(TENSOR)
    f_index = lax.axis_index(FSDP)
    t_index = lax.axis_index(TENSOR)
    block_rows, full_width = old_codes.shape
    col_width = full_width // n_fsdp
    col_tiles = col_width // TILE
    per_owner = n_fsdp // n_tensor
    own_rows = block_rows * n_fsdp
    row_tiles = own_rows // TILE
    hidden = (jax.nn.silu(gate_pre.astype(jnp.float32)) * up_pre.astype(jnp.float32)).astype(
        jnp.bfloat16
    )
    near = lax.all_gather(hidden, "h", axis=0, tiled=True)
    every = lax.all_gather(near, "z", axis=0, tiled=True)
    sectioned = lax.all_to_all(old_codes, FSDP, split_axis=1, concat_axis=0, tiled=True)
    moved = lax.all_to_all(
        sectioned.reshape(n_tensor, per_owner * block_rows, col_width),
        TENSOR,
        split_axis=0,
        concat_axis=0,
        tiled=True,
    )
    final_rows = jnp.swapaxes(
        moved.reshape(n_tensor, per_owner, block_rows, col_width), 0, 1
    ).reshape(own_rows, col_width)
    scale_block = lax.dynamic_slice(
        old_scales, (t_index * row_tiles, f_index * col_tiles), (row_tiles, col_tiles)
    )
    tile_values = (
        final_rows.astype(jnp.float32).reshape(row_tiles, TILE, col_tiles, TILE)
        * scale_block[:, None, :, None]
    )
    new_scale = jnp.max(jnp.abs(tile_values), axis=(1, 3)) + EPSILON
    new_codes = (tile_values / new_scale[:, None, :, None]).astype(jnp.bfloat16)
    weight = (
        (new_codes.astype(jnp.float32) * new_scale[:, None, :, None])
        .astype(jnp.bfloat16)
        .reshape(own_rows, col_width)
    )
    partial_value = jnp.dot(every, weight, preferred_element_type=jnp.float32)
    codes_t = new_codes.reshape(own_rows, col_width).T
    scales_t = new_scale.T
    shares = lax.all_to_all(
        partial_value.astype(jnp.bfloat16), TENSOR, split_axis=0, concat_axis=0, tiled=True
    )
    tokens = shares.shape[0] // n_tensor
    mixed = jnp.sum(
        shares.reshape(n_tensor, tokens, col_width).astype(jnp.float32), axis=0
    ).astype(jnp.bfloat16)
    return (mixed, codes_t, scales_t)


def solution(mesh):
    fine = Mesh(mesh.devices.reshape(SIZES), AXES)
    return jax.shard_map(
        body,
        mesh=fine,
        in_specs=(P(FSDP + TENSOR, None), P(), P(FSDP, TENSOR), P(FSDP, TENSOR)),
        out_specs=(P(TENSOR, FSDP), P(FSDP, TENSOR), P(FSDP, TENSOR)),
        check_vma=False,
    )
```

```python
import jax
import jax.numpy as jnp
from jax import lax
from jax.experimental import pallas as pl
from jax.experimental.pallas import tpu as pltpu
from jax.sharding import Mesh, PartitionSpec as P

TILE = 128
EPSILON = 1e-06
AXES = ("z", "h", "x", "l", "c")
SIZES = (8, 4, 4, 2, 2)
FSDP = ("z", "h")
TENSOR = ("x", "l", "c")
PACK_STEPS = 4


def pack_kernel(in_ref, out_ref, scratch):
    rows = in_ref.shape[0]
    sections, _, lanes = out_ref.shape
    tiles = in_ref.shape[1] // (sections * lanes)
    for section in range(sections):
        for tile in range(tiles):
            at = (section * tiles + tile) * lanes
            scratch[pl.ds(tile * rows, rows), :] = in_ref[:, pl.ds(at, lanes)].astype(jnp.float32)
        out_ref[section] = scratch[...].astype(jnp.bfloat16)


def pack(old_codes, n_fsdp):
    rows, width = old_codes.shape
    packed_rows = rows * width // n_fsdp // TILE
    sections = n_fsdp // PACK_STEPS
    return pl.pallas_call(
        pack_kernel,
        out_shape=jax.ShapeDtypeStruct((n_fsdp, packed_rows, TILE), jnp.bfloat16),
        grid=(PACK_STEPS,),
        in_specs=[pl.BlockSpec((rows, width // PACK_STEPS), lambda i: (0, i))],
        out_specs=pl.BlockSpec((sections, packed_rows, TILE), lambda i: (i, 0, 0)),
        scratch_shapes=[pltpu.VMEM((packed_rows, TILE), jnp.float32)],
        compiler_params=pltpu.CompilerParams(vmem_limit_bytes=12 << 20),
        name="pack",
    )(old_codes)


def requantize_kernel(scale_ref, in_ref, codes_ref, weight_ref, new_scale_ref, rows_ref, piece_ref):
    senders, parts, packed_rows, _ = in_ref.shape
    total_rows, width = rows_ref.shape
    tiles = width // TILE
    rows = packed_rows // tiles

    for part in range(parts):
        for sender in range(senders):
            slot = sender % 2
            piece_ref[slot] = in_ref[sender, part].astype(jnp.float32)
            base = (part * senders + sender) * rows
            for tile in range(tiles):
                rows_ref[pl.ds(base, rows), tile * TILE : (tile + 1) * TILE] = piece_ref[
                    slot, pl.ds(tile * rows, rows), :
                ]
    lane = lax.broadcasted_iota(jnp.int32, (1, TILE), 1)

    def one_row(row, carry):
        at = pl.ds(pl.multiple_of(row * TILE, TILE), TILE)
        line = jnp.zeros((1, TILE), jnp.float32)
        for tile in range(tiles):
            cols = slice(tile * TILE, (tile + 1) * TILE)
            codes = rows_ref[at, cols]
            scale = scale_ref[row, tile]
            top = jnp.max(jnp.abs(codes), axis=0, keepdims=True)
            new_scale = jnp.max(top, axis=1, keepdims=True) * scale + EPSILON
            line = jnp.where(lane == tile, new_scale, line)
            new_codes = (codes * scale / new_scale).astype(jnp.bfloat16)
            codes_ref[at, cols] = new_codes
            weight_ref[at, cols] = (new_codes.astype(jnp.float32) * new_scale).astype(jnp.bfloat16)
        new_scale_ref[pl.ds(row, 1), :] = line
        return carry

    lax.fori_loop(0, total_rows // TILE, one_row, 0)


def requantize(moved, scale_block, width):
    senders, parts, packed_rows, _ = moved.shape
    total_rows = senders * parts * packed_rows * TILE // width
    vmem = pl.BlockSpec(memory_space=pltpu.VMEM)
    return pl.pallas_call(
        requantize_kernel,
        out_shape=(
            jax.ShapeDtypeStruct((total_rows, width), jnp.bfloat16),
            jax.ShapeDtypeStruct((total_rows, width), jnp.bfloat16),
            jax.ShapeDtypeStruct((total_rows // TILE, TILE), jnp.float32),
        ),
        in_specs=[pl.BlockSpec(memory_space=pltpu.SMEM), vmem],
        out_specs=(vmem, vmem, vmem),
        scratch_shapes=[
            pltpu.VMEM((total_rows, width), jnp.float32),
            pltpu.VMEM((2, packed_rows, TILE), jnp.float32),
        ],
        compiler_params=pltpu.CompilerParams(vmem_limit_bytes=20 << 20),
        name="requantize",
    )(scale_block, moved)


def body(old_codes, old_scales, gate_pre, up_pre):
    n_fsdp = lax.axis_size(FSDP)
    n_tensor = lax.axis_size(TENSOR)
    f_index = lax.axis_index(FSDP)
    t_index = lax.axis_index(TENSOR)
    block_rows, full_width = old_codes.shape
    col_width = full_width // n_fsdp
    col_tiles = col_width // TILE
    per_owner = n_fsdp // n_tensor
    own_rows = block_rows * n_fsdp
    row_tiles = own_rows // TILE
    hidden = (jax.nn.silu(gate_pre.astype(jnp.float32)) * up_pre.astype(jnp.float32)).astype(
        jnp.bfloat16
    )
    half = hidden.shape[0] // 2
    first = lax.all_gather(hidden[:half], FSDP, axis=0, tiled=True)
    packed = pack(old_codes, n_fsdp)
    packed_rows = packed.shape[1]
    near = lax.all_gather(hidden[half:], "h", axis=0, tiled=True)
    second = lax.all_gather(near, "z", axis=0, tiled=True)

    sectioned = lax.all_to_all(packed, FSDP, split_axis=0, concat_axis=0, tiled=True)
    moved = lax.all_to_all(
        sectioned.reshape(n_tensor, per_owner * packed_rows, TILE),
        TENSOR,
        split_axis=0,
        concat_axis=0,
        tiled=True,
    )
    scale_block = lax.dynamic_slice(
        old_scales, (t_index * row_tiles, f_index * col_tiles), (row_tiles, col_tiles)
    )
    new_codes, weight, new_scale = requantize(
        moved.reshape(n_tensor, per_owner, packed_rows, TILE), scale_block, col_width
    )
    codes_t = new_codes.T
    scales_t = new_scale[:, :col_tiles].T

    pieces = []
    for tokens in (first, second):
        share = jnp.dot(tokens, weight, preferred_element_type=jnp.float32).astype(jnp.bfloat16)
        shares = lax.all_to_all(share, TENSOR, split_axis=0, concat_axis=0, tiled=True)
        total = jnp.sum(
            shares.reshape(n_tensor, per_owner, half, col_width).astype(jnp.float32), axis=0
        )
        pieces.append(total.astype(jnp.bfloat16))
    mixed = jnp.stack(pieces, axis=1).reshape(per_owner * 2 * half, col_width)
    return (mixed, codes_t, scales_t)


def solution(mesh):
    fine = Mesh(mesh.devices.reshape(SIZES), AXES)
    return jax.shard_map(
        body,
        mesh=fine,
        in_specs=(P(FSDP + TENSOR, None), P(), P(FSDP, TENSOR), P(FSDP, TENSOR)),
        out_specs=(P(TENSOR, FSDP), P(FSDP, TENSOR), P(FSDP, TENSOR)),
        check_vma=False,
    )
```

```python
import functools

import jax
import jax.numpy as jnp
from jax import lax
from jax.experimental import pallas as pl
from jax.experimental.pallas import tpu as pltpu
from jax.sharding import Mesh, PartitionSpec as P

TILE = 128
EPSILON = 1e-06
AXES = ("z", "h", "x", "l", "c")
SIZES = (8, 4, 4, 2, 2)
FSDP = ("z", "h")
TENSOR = ("x", "l", "c")
PACK_STEPS = 4


def pack_kernel(in_ref, out_ref, scratch):
    rows = in_ref.shape[0]
    sections, _, lanes = out_ref.shape
    tiles = in_ref.shape[1] // (sections * lanes)
    for section in range(sections):
        for tile in range(tiles):
            at = (section * tiles + tile) * lanes
            scratch[pl.ds(tile * rows, rows), :] = in_ref[:, pl.ds(at, lanes)].astype(jnp.float32)
        out_ref[section] = scratch[...].astype(jnp.bfloat16)


def pack(old_codes, n_fsdp):
    rows, width = old_codes.shape
    packed_rows = rows * width // n_fsdp // TILE
    sections = n_fsdp // PACK_STEPS
    return pl.pallas_call(
        pack_kernel,
        out_shape=jax.ShapeDtypeStruct((n_fsdp, packed_rows, TILE), jnp.bfloat16),
        grid=(PACK_STEPS,),
        in_specs=[pl.BlockSpec((rows, width // PACK_STEPS), lambda i: (0, i))],
        out_specs=pl.BlockSpec((sections, packed_rows, TILE), lambda i: (i, 0, 0)),
        scratch_shapes=[pltpu.VMEM((packed_rows, TILE), jnp.float32)],
        compiler_params=pltpu.CompilerParams(vmem_limit_bytes=12 << 20),
        name="pack",
    )(old_codes)


def requantize_kernel(scale_ref, in_ref, codes_ref, weight_ref, new_scale_ref, rows_ref, piece_ref):
    senders, parts, packed_rows, _ = in_ref.shape
    total_rows, width = rows_ref.shape
    tiles = width // TILE
    rows = packed_rows // tiles

    for part in range(parts):
        for sender in range(senders):
            slot = sender % 2
            piece_ref[slot] = in_ref[sender, part].astype(jnp.float32)
            base = (part * senders + sender) * rows
            for tile in range(tiles):
                rows_ref[pl.ds(base, rows), tile * TILE : (tile + 1) * TILE] = piece_ref[
                    slot, pl.ds(tile * rows, rows), :
                ]
    lane = lax.broadcasted_iota(jnp.int32, (1, TILE), 1)

    def one_row(row, carry):
        at = pl.ds(pl.multiple_of(row * TILE, TILE), TILE)
        line = jnp.zeros((1, TILE), jnp.float32)
        for tile in range(tiles):
            cols = slice(tile * TILE, (tile + 1) * TILE)
            codes = rows_ref[at, cols]
            scale = scale_ref[row, tile]
            top = jnp.max(jnp.abs(codes), axis=0, keepdims=True)
            new_scale = jnp.max(top, axis=1, keepdims=True) * scale + EPSILON
            line = jnp.where(lane == tile, new_scale, line)
            new_codes = (codes * scale / new_scale).astype(jnp.bfloat16)
            codes_ref[at, cols] = new_codes
            weight_ref[at, cols] = (new_codes.astype(jnp.float32) * new_scale).astype(jnp.bfloat16)
        new_scale_ref[pl.ds(row, 1), :] = line
        return carry

    lax.fori_loop(0, total_rows // TILE, one_row, 0)


def requantize(moved, scale_block, width):
    senders, parts, packed_rows, _ = moved.shape
    total_rows = senders * parts * packed_rows * TILE // width
    vmem = pl.BlockSpec(memory_space=pltpu.VMEM)
    return pl.pallas_call(
        requantize_kernel,
        out_shape=(
            jax.ShapeDtypeStruct((total_rows, width), jnp.bfloat16),
            jax.ShapeDtypeStruct((total_rows, width), jnp.bfloat16),
            jax.ShapeDtypeStruct((total_rows // TILE, TILE), jnp.float32),
        ),
        in_specs=[pl.BlockSpec(memory_space=pltpu.SMEM), vmem],
        out_specs=(vmem, vmem, vmem),
        scratch_shapes=[
            pltpu.VMEM((total_rows, width), jnp.float32),
            pltpu.VMEM((2, packed_rows, TILE), jnp.float32),
        ],
        compiler_params=pltpu.CompilerParams(vmem_limit_bytes=16 << 20),
        name="requantize",
    )(scale_block, moved)


def product_kernel(n_z, n_h, rows, places, at_ref, *refs):
    *block_refs, weight_ref, out_ref, tokens_ref = refs
    for (shift, first), block_ref in zip(places, block_refs):
        z_from = lax.rem(at_ref[0] + shift, n_z)
        for group in range(block_ref.shape[0] // rows):
            h_from = lax.rem(at_ref[1] + first + group, n_h)
            place = pl.multiple_of((z_from * n_h + h_from) * rows, rows)
            tokens_ref[pl.ds(place, rows), :] = block_ref[group * rows : (group + 1) * rows, :]
    part = 256
    for at in range(0, tokens_ref.shape[0], part):
        out_ref[at : at + part, :] = jnp.dot(
            tokens_ref[at : at + part, :], weight_ref[...], preferred_element_type=jnp.float32
        ).astype(jnp.bfloat16)


def product(at, places, blocks, weight, n_z, n_h):
    depth, width = weight.shape
    count = sum(block.shape[0] for block in blocks)
    vmem = pl.BlockSpec(memory_space=pltpu.VMEM)
    return pl.pallas_call(
        functools.partial(product_kernel, n_z, n_h, count // (n_z * n_h), places),
        out_shape=jax.ShapeDtypeStruct((count, width), jnp.bfloat16),
        in_specs=[pl.BlockSpec(memory_space=pltpu.SMEM)] + [vmem] * (len(blocks) + 1),
        out_specs=vmem,
        scratch_shapes=[pltpu.VMEM((count, depth), jnp.bfloat16)],
        compiler_params=pltpu.CompilerParams(vmem_limit_bytes=16 << 20),
        cost_estimate=pl.CostEstimate(
            flops=2 * count * depth * width,
            bytes_accessed=2 * (count * depth + depth * width + count * width),
            transcendentals=0,
        ),
        name="product",
    )(at, *blocks, weight)


def rings(leading, trailing, weight, n_z):
    up = [(i, (i + 1) % n_z) for i in range(n_z)]
    down = [(i, (i - 1) % n_z) for i in range(n_z)]
    rows = leading.shape[0] // 2
    steps = n_z // 2

    def advance(pair, step):
        below, above = pair
        if step == steps:
            below, above = below[:rows], above[rows:]
        return lax.ppermute(below, "z", up), lax.ppermute(above, "z", down)

    lead, trail = [(leading, leading)], [(trailing, trailing)]
    for step in range(1, steps + 1):
        if step > 2:
            also = (weight,) if step == steps else ()
            tied = lax.optimization_barrier(lead[-1] + trail[-1] + also)
            lead[-1], trail[-1] = tied[:2], tied[2:4]
            weight = tied[4] if also else weight
        lead.append(advance(lead[-1], step))
        if step < steps - 1:
            trail.append(advance(trail[-1], step))
    trail.append(advance(trail[-1], steps - 1))
    tied = lax.optimization_barrier(lead[-1] + trail[-1])
    lead[-1], trail[-1] = tied[:2], tied[2:]
    trail.append(advance(trail[-1], steps))
    places = [(0, 0)]
    for step in range(1, steps + 1):
        places += [(n_z - step, 0), (step, 2 if step == steps else 0)]
    leading_blocks = [leading] + [block for pair in lead[1:] for block in pair]
    trailing_blocks = [trailing] + [block for pair in trail[1:] for block in pair]
    return tuple(places), leading_blocks, trailing_blocks, weight


def body(old_codes, old_scales, gate_pre, up_pre):
    n_fsdp = lax.axis_size(FSDP)
    n_tensor = lax.axis_size(TENSOR)
    f_index = lax.axis_index(FSDP)
    t_index = lax.axis_index(TENSOR)
    block_rows, full_width = old_codes.shape
    col_width = full_width // n_fsdp
    col_tiles = col_width // TILE
    per_owner = n_fsdp // n_tensor
    own_rows = block_rows * n_fsdp
    row_tiles = own_rows // TILE
    hidden = (jax.nn.silu(gate_pre.astype(jnp.float32)) * up_pre.astype(jnp.float32)).astype(
        jnp.bfloat16
    )
    n_z = lax.axis_size("z")
    n_h = lax.axis_size("h")
    at = jnp.stack([lax.axis_index("z"), lax.axis_index("h")]).astype(jnp.int32)
    half = hidden.shape[0] // 2
    beside = [hidden]
    for step in range(1, n_h):
        pairs = [(i, (i - step) % n_h) for i in range(n_h)]
        beside.append(lax.ppermute(hidden, "h", pairs))
    halves = [
        jnp.concatenate([block[part * half : (part + 1) * half] for block in beside])
        for part in range(2)
    ]
    packed = pack(old_codes, n_fsdp)
    packed_rows = packed.shape[1]

    sectioned = lax.all_to_all(packed, FSDP, split_axis=0, concat_axis=0, tiled=True)
    moved = lax.all_to_all(
        sectioned.reshape(n_tensor, per_owner * packed_rows, TILE),
        TENSOR,
        split_axis=0,
        concat_axis=0,
        tiled=True,
    )
    scale_block = lax.dynamic_slice(
        old_scales, (t_index * row_tiles, f_index * col_tiles), (row_tiles, col_tiles)
    )
    new_codes, weight, new_scale = requantize(
        moved.reshape(n_tensor, per_owner, packed_rows, TILE), scale_block, col_width
    )
    codes_t = new_codes.T
    scales_t = new_scale[:, :col_tiles].T

    places, blocks_one, blocks_two, weight = rings(halves[0], halves[1], weight, n_z)
    pieces = []
    for blocks in (blocks_one, blocks_two):
        share = product(at, places, blocks, weight, n_z, n_h)
        shares = lax.all_to_all(share, TENSOR, split_axis=0, concat_axis=0, tiled=True)
        total = jnp.sum(
            shares.reshape(n_tensor, per_owner, half, col_width).astype(jnp.float32), axis=0
        )
        pieces.append(total.astype(jnp.bfloat16))
    mixed = jnp.stack(pieces, axis=1).reshape(per_owner * 2 * half, col_width)
    return (mixed, codes_t, scales_t)


def solution(mesh):
    fine = Mesh(mesh.devices.reshape(SIZES), AXES)
    return jax.shard_map(
        body,
        mesh=fine,
        in_specs=(P(FSDP + TENSOR, None), P(), P(FSDP, TENSOR), P(FSDP, TENSOR)),
        out_specs=(P(TENSOR, FSDP), P(FSDP, TENSOR), P(FSDP, TENSOR)),
        check_vma=False,
    )
```

```python
import functools

import jax
import jax.numpy as jnp
from jax import lax
from jax.experimental import pallas as pl
from jax.experimental.pallas import tpu as pltpu
from jax.sharding import Mesh, PartitionSpec as P

TILE = 128
EPSILON = 1e-06
AXES = ("z", "h", "x", "l", "c")
SIZES = (8, 4, 4, 2, 2)
FSDP = ("z", "h")
TENSOR = ("x", "l", "c")
PACK_STEPS = 4
OUTER = 16
INNER = 16


def pack_kernel(in_ref, out_ref, scratch):
    rows = in_ref.shape[0]
    sections, _, lanes = out_ref.shape
    tiles = in_ref.shape[1] // (sections * lanes)
    for section in range(sections):
        for tile in range(tiles):
            at = (section * tiles + tile) * lanes
            scratch[pl.ds(tile * rows, rows), :] = in_ref[:, pl.ds(at, lanes)].astype(jnp.float32)
        out_ref[section] = scratch[...].astype(jnp.bfloat16)


def pack(old_codes, n_fsdp):
    rows, width = old_codes.shape
    packed_rows = rows * width // n_fsdp // TILE
    sections = n_fsdp // PACK_STEPS
    return pl.pallas_call(
        pack_kernel,
        out_shape=jax.ShapeDtypeStruct((n_fsdp, packed_rows, TILE), jnp.bfloat16),
        grid=(PACK_STEPS,),
        in_specs=[pl.BlockSpec((rows, width // PACK_STEPS), lambda i: (0, i))],
        out_specs=pl.BlockSpec((sections, packed_rows, TILE), lambda i: (i, 0, 0)),
        scratch_shapes=[pltpu.VMEM((packed_rows, TILE), jnp.float32)],
        compiler_params=pltpu.CompilerParams(vmem_limit_bytes=12 << 20),
        name="pack",
    )(old_codes)


def requantize_kernel(scale_ref, in_ref, codes_ref, weight_ref, new_scale_ref, rows_ref, piece_ref):
    senders, parts, packed_rows, _ = in_ref.shape
    total_rows, width = rows_ref.shape
    tiles = width // TILE
    rows = packed_rows // tiles

    for part in range(parts):
        for sender in range(senders):
            slot = sender % 2
            piece_ref[slot] = in_ref[sender, part].astype(jnp.float32)
            base = (part * senders + sender) * rows
            for tile in range(tiles):
                rows_ref[pl.ds(base, rows), tile * TILE : (tile + 1) * TILE] = piece_ref[
                    slot, pl.ds(tile * rows, rows), :
                ]
    lane = lax.broadcasted_iota(jnp.int32, (1, TILE), 1)

    def one_row(row, carry):
        at = pl.ds(pl.multiple_of(row * TILE, TILE), TILE)
        line = jnp.zeros((1, TILE), jnp.float32)
        for tile in range(tiles):
            cols = slice(tile * TILE, (tile + 1) * TILE)
            codes = rows_ref[at, cols]
            scale = scale_ref[row, tile]
            top = jnp.max(jnp.abs(codes), axis=0, keepdims=True)
            new_scale = jnp.max(top, axis=1, keepdims=True) * scale + EPSILON
            line = jnp.where(lane == tile, new_scale, line)
            new_codes = (codes * scale / new_scale).astype(jnp.bfloat16)
            codes_ref[at, cols] = new_codes
            weight_ref[at, cols] = (new_codes.astype(jnp.float32) * new_scale).astype(jnp.bfloat16)
        new_scale_ref[pl.ds(row, 1), :] = line
        return carry

    lax.fori_loop(0, total_rows // TILE, one_row, 0)


def requantize(moved, scale_block, width):
    senders, parts, packed_rows, _ = moved.shape
    total_rows = senders * parts * packed_rows * TILE // width
    vmem = pl.BlockSpec(memory_space=pltpu.VMEM)
    return pl.pallas_call(
        requantize_kernel,
        out_shape=(
            jax.ShapeDtypeStruct((total_rows, width), jnp.bfloat16),
            jax.ShapeDtypeStruct((total_rows, width), jnp.bfloat16),
            jax.ShapeDtypeStruct((total_rows // TILE, TILE), jnp.float32),
        ),
        in_specs=[pl.BlockSpec(memory_space=pltpu.SMEM), vmem],
        out_specs=(vmem, vmem, vmem),
        scratch_shapes=[
            pltpu.VMEM((total_rows, width), jnp.float32),
            pltpu.VMEM((2, packed_rows, TILE), jnp.float32),
        ],
        compiler_params=pltpu.CompilerParams(vmem_limit_bytes=20 << 20),
        name="requantize",
    )(scale_block, moved)


def product_kernel(n_z, n_h, early_ref, late_ref, first_ref, weight_ref, out_ref):
    sections = n_z * n_h
    rows = out_ref.shape[0] // sections
    outer = early_ref.shape[0] * 2 // sections
    inner = rows - outer
    for which, ref in enumerate((early_ref, late_ref)):
        value = jnp.dot(ref[...], weight_ref[...], preferred_element_type=jnp.float32)
        value = value.astype(jnp.bfloat16)
        for h in range(n_h):
            for z in range(n_z // 2):
                at = ((which * (n_z // 2) + z) * n_h + h) * rows
                source = (h * (n_z // 2) + z) * outer
                out_ref[at : at + outer, :] = value[source : source + outer, :]
    part = n_z // 2 * n_h * inner
    for which in range(2):
        value = jnp.dot(
            first_ref[which * part : (which + 1) * part, :],
            weight_ref[...],
            preferred_element_type=jnp.float32,
        ).astype(jnp.bfloat16)
        for section in range(sections // 2):
            at = (which * (sections // 2) + section) * rows + outer
            out_ref[at : at + inner, :] = value[section * inner : (section + 1) * inner, :]


def product(early, late, first, weight, n_z, n_h):
    depth, width = weight.shape
    count = early.shape[0] + late.shape[0] + first.shape[0]
    vmem = pl.BlockSpec(memory_space=pltpu.VMEM)
    return pl.pallas_call(
        functools.partial(product_kernel, n_z, n_h),
        out_shape=jax.ShapeDtypeStruct((count, width), jnp.bfloat16),
        in_specs=[vmem] * 4,
        out_specs=vmem,
        compiler_params=pltpu.CompilerParams(vmem_limit_bytes=20 << 20),
        cost_estimate=pl.CostEstimate(
            flops=2 * count * depth * width,
            bytes_accessed=2 * (count * depth + depth * width + count * width),
            transcendentals=0,
        ),
        name="product",
    )(early, late, first, weight)


def body(old_codes, old_scales, gate_pre, up_pre):
    n_fsdp = lax.axis_size(FSDP)
    n_tensor = lax.axis_size(TENSOR)
    f_index = lax.axis_index(FSDP)
    t_index = lax.axis_index(TENSOR)
    block_rows, full_width = old_codes.shape
    col_width = full_width // n_fsdp
    col_tiles = col_width // TILE
    per_owner = n_fsdp // n_tensor
    own_rows = block_rows * n_fsdp
    row_tiles = own_rows // TILE
    hidden = (jax.nn.silu(gate_pre.astype(jnp.float32)) * up_pre.astype(jnp.float32)).astype(
        jnp.bfloat16
    )
    n_z = lax.axis_size("z")
    n_h = lax.axis_size("h")
    packed = pack(old_codes, n_fsdp)
    packed_rows = packed.shape[1]
    sectioned = lax.all_to_all(packed, FSDP, split_axis=0, concat_axis=0, tiled=True)
    near = lax.all_gather(hidden[OUTER:], "h", axis=0, tiled=True)
    far = lax.all_gather(hidden[:OUTER], "z", axis=0, tiled=True)
    parted = near.reshape(n_h, -1, own_rows)
    one = parted[:, :INNER].reshape(-1, own_rows)
    two = parted[:, INNER:].reshape(-1, own_rows)
    one, two, far, sectioned = lax.optimization_barrier((one, two, far, sectioned))
    first = lax.all_gather(one, "z", axis=0, tiled=True)
    second = lax.all_gather(two, "z", axis=0, tiled=True)
    middle = far.shape[0] // 2
    early = lax.all_gather(far[:middle], "h", axis=0, tiled=True)
    late = lax.all_gather(far[middle:], "h", axis=0, tiled=True)
    moved = lax.all_to_all(
        sectioned.reshape(n_tensor, per_owner * packed_rows, TILE),
        TENSOR,
        split_axis=0,
        concat_axis=0,
        tiled=True,
    )
    moved, early, late = lax.optimization_barrier((moved, early, late))
    scale_block = lax.dynamic_slice(
        old_scales, (t_index * row_tiles, f_index * col_tiles), (row_tiles, col_tiles)
    )
    new_codes, weight, new_scale = requantize(
        moved.reshape(n_tensor, per_owner, packed_rows, TILE), scale_block, col_width
    )
    codes_t = new_codes.T
    scales_t = new_scale[:, :col_tiles].T

    def reduced(share):
        shares = lax.all_to_all(share, TENSOR, split_axis=0, concat_axis=0, tiled=True)
        total = jnp.sum(shares.reshape(n_tensor, -1, col_width).astype(jnp.float32), axis=0)
        return total.astype(jnp.bfloat16).reshape(per_owner, -1, col_width)

    lead = reduced(product(early, late, first, weight, n_z, n_h))
    trail = reduced(jnp.dot(second, weight, preferred_element_type=jnp.float32).astype(jnp.bfloat16))
    mixed = jnp.concatenate([lead, trail], axis=1).reshape(-1, col_width)
    return (mixed, codes_t, scales_t)


def solution(mesh):
    fine = Mesh(mesh.devices.reshape(SIZES), AXES)
    return jax.shard_map(
        body,
        mesh=fine,
        in_specs=(P(FSDP + TENSOR, None), P(), P(FSDP, TENSOR), P(FSDP, TENSOR)),
        out_specs=(P(TENSOR, FSDP), P(FSDP, TENSOR), P(FSDP, TENSOR)),
        check_vma=False,
    )
```

```python
import jax
import jax.numpy as jnp
from jax import lax
from jax.experimental import pallas as pl
from jax.experimental.pallas import tpu as pltpu
from jax.sharding import Mesh, PartitionSpec as P

TILE = 128
EPSILON = 1e-06
AXES = ("z", "h", "x", "l", "c")
SIZES = (8, 4, 4, 2, 2)
FSDP = ("z", "h")
TENSOR = ("x", "l", "c")
PACK_STEPS = 4


def pack_kernel(in_ref, out_ref, scratch):
    rows = in_ref.shape[0]
    sections, _, lanes = out_ref.shape
    tiles = in_ref.shape[1] // (sections * lanes)
    for section in range(sections):
        for tile in range(tiles):
            at = (section * tiles + tile) * lanes
            scratch[pl.ds(tile * rows, rows), :] = in_ref[:, pl.ds(at, lanes)].astype(jnp.float32)
        out_ref[section] = scratch[...].astype(jnp.bfloat16)


def pack(old_codes, n_fsdp):
    rows, width = old_codes.shape
    packed_rows = rows * width // n_fsdp // TILE
    sections = n_fsdp // PACK_STEPS
    return pl.pallas_call(
        pack_kernel,
        out_shape=jax.ShapeDtypeStruct((n_fsdp, packed_rows, TILE), jnp.bfloat16),
        grid=(PACK_STEPS,),
        in_specs=[pl.BlockSpec((rows, width // PACK_STEPS), lambda i: (0, i))],
        out_specs=pl.BlockSpec((sections, packed_rows, TILE), lambda i: (i, 0, 0)),
        scratch_shapes=[pltpu.VMEM((packed_rows, TILE), jnp.float32)],
        compiler_params=pltpu.CompilerParams(vmem_limit_bytes=12 << 20),
        name="pack",
    )(old_codes)


def requantize_kernel(scale_ref, in_ref, codes_ref, weight_ref, new_scale_ref, rows_ref, piece_ref):
    senders, parts, packed_rows, _ = in_ref.shape
    total_rows, width = rows_ref.shape
    tiles = width // TILE
    rows = packed_rows // tiles

    for part in range(parts):
        for sender in range(senders):
            slot = sender % 2
            piece_ref[slot] = in_ref[sender, part].astype(jnp.float32)
            base = (part * senders + sender) * rows
            for tile in range(tiles):
                rows_ref[pl.ds(base, rows), tile * TILE : (tile + 1) * TILE] = piece_ref[
                    slot, pl.ds(tile * rows, rows), :
                ]
    lane = lax.broadcasted_iota(jnp.int32, (1, TILE), 1)

    def one_row(row, carry):
        at = pl.ds(pl.multiple_of(row * TILE, TILE), TILE)
        line = jnp.zeros((1, TILE), jnp.float32)
        for tile in range(tiles):
            cols = slice(tile * TILE, (tile + 1) * TILE)
            codes = rows_ref[at, cols]
            scale = scale_ref[row, tile]
            top = jnp.max(jnp.abs(codes), axis=0, keepdims=True)
            new_scale = jnp.max(top, axis=1, keepdims=True) * scale + EPSILON
            line = jnp.where(lane == tile, new_scale, line)
            new_codes = (codes * scale / new_scale).astype(jnp.bfloat16)
            codes_ref[at, cols] = new_codes
            weight_ref[at, cols] = (new_codes.astype(jnp.float32) * new_scale).astype(jnp.bfloat16)
        new_scale_ref[pl.ds(row, 1), :] = line
        return carry

    lax.fori_loop(0, total_rows // TILE, one_row, 0)


def requantize(moved, scale_block, width):
    senders, parts, packed_rows, _ = moved.shape
    total_rows = senders * parts * packed_rows * TILE // width
    vmem = pl.BlockSpec(memory_space=pltpu.VMEM)
    return pl.pallas_call(
        requantize_kernel,
        out_shape=(
            jax.ShapeDtypeStruct((total_rows, width), jnp.bfloat16),
            jax.ShapeDtypeStruct((total_rows, width), jnp.bfloat16),
            jax.ShapeDtypeStruct((total_rows // TILE, TILE), jnp.float32),
        ),
        in_specs=[pl.BlockSpec(memory_space=pltpu.SMEM), vmem],
        out_specs=(vmem, vmem, vmem),
        scratch_shapes=[
            pltpu.VMEM((total_rows, width), jnp.float32),
            pltpu.VMEM((2, packed_rows, TILE), jnp.float32),
        ],
        compiler_params=pltpu.CompilerParams(vmem_limit_bytes=20 << 20),
        name="requantize",
    )(scale_block, moved)


def body(old_codes, old_scales, gate_pre, up_pre):
    n_fsdp = lax.axis_size(FSDP)
    n_tensor = lax.axis_size(TENSOR)
    f_index = lax.axis_index(FSDP)
    t_index = lax.axis_index(TENSOR)
    block_rows, full_width = old_codes.shape
    col_width = full_width // n_fsdp
    col_tiles = col_width // TILE
    per_owner = n_fsdp // n_tensor
    own_rows = block_rows * n_fsdp
    row_tiles = own_rows // TILE
    hidden = (jax.nn.silu(gate_pre.astype(jnp.float32)) * up_pre.astype(jnp.float32)).astype(
        jnp.bfloat16
    )
    n_z = lax.axis_size("z")
    n_h = lax.axis_size("h")
    near = lax.all_gather(hidden, "h", axis=0, tiled=True)
    packed = pack(old_codes, n_fsdp)
    packed_rows = packed.shape[1]

    def swapped(sections, rows):
        return jnp.swapaxes(sections.reshape(rows, -1, packed_rows, TILE), 0, 1).reshape(
            n_fsdp, packed_rows, TILE
        )

    along_z = lax.all_to_all(packed, "z", split_axis=0, concat_axis=0, tiled=True)
    near, along_z = lax.optimization_barrier((near, along_z))
    every = lax.all_gather(near, "z", axis=0, tiled=True)
    sectioned = lax.all_to_all(swapped(along_z, n_z), "h", split_axis=0, concat_axis=0, tiled=True)
    moved = lax.all_to_all(
        swapped(sectioned, n_h).reshape(n_tensor, per_owner * packed_rows, TILE),
        TENSOR,
        split_axis=0,
        concat_axis=0,
        tiled=True,
    )
    scale_block = lax.dynamic_slice(
        old_scales, (t_index * row_tiles, f_index * col_tiles), (row_tiles, col_tiles)
    )
    new_codes, weight, new_scale = requantize(
        moved.reshape(n_tensor, per_owner, packed_rows, TILE), scale_block, col_width
    )
    codes_t = new_codes.T
    scales_t = new_scale[:, :col_tiles].T

    n_c = lax.axis_size("c")
    core = lax.axis_index("c")
    share = jnp.dot(every, weight, preferred_element_type=jnp.float32).astype(jnp.bfloat16)
    by_core = share.reshape(n_tensor // n_c, n_c, -1, col_width)
    other = lax.dynamic_index_in_dim(by_core, 1 - core, 1, keepdims=False)
    other = lax.ppermute(other, "c", [(0, 1), (1, 0)])
    own = lax.dynamic_index_in_dim(by_core, core, 1, keepdims=False)
    share = (own.astype(jnp.float32) + other.astype(jnp.float32)).astype(jnp.bfloat16)
    shares = lax.all_to_all(share, ("x", "l"), split_axis=0, concat_axis=0, tiled=True)
    mixed = jnp.sum(
        shares.reshape(n_tensor // n_c, -1, col_width).astype(jnp.float32), axis=0
    ).astype(jnp.bfloat16)
    return (mixed, codes_t, scales_t)


def solution(mesh):
    fine = Mesh(mesh.devices.reshape(SIZES), AXES)
    return jax.shard_map(
        body,
        mesh=fine,
        in_specs=(P(FSDP + TENSOR, None), P(), P(FSDP, TENSOR), P(FSDP, TENSOR)),
        out_specs=(P(TENSOR, FSDP), P(FSDP, TENSOR), P(FSDP, TENSOR)),
        check_vma=False,
    )
```

```python
import itertools
import math

import jax
import jax.numpy as jnp
from jax import lax
from jax.experimental import pallas as pl
from jax.experimental.pallas import tpu as pltpu
from jax.sharding import Mesh, PartitionSpec as P

TILE = 128
EPSILON = 1e-06
AXES = ("z", "h", "x", "l", "c")
SIZES = (8, 4, 4, 2, 2)
FSDP = ("z", "h")
TENSOR = ("x", "l", "c")
PACK_STEPS = 4


def pack_kernel(in_ref, out_ref, scratch):
    rows = in_ref.shape[0]
    sections, _, lanes = out_ref.shape
    tiles = in_ref.shape[1] // (sections * lanes)
    for section in range(sections):
        for tile in range(tiles):
            at = (section * tiles + tile) * lanes
            scratch[pl.ds(tile * rows, rows), :] = in_ref[:, pl.ds(at, lanes)].astype(jnp.float32)
        out_ref[section] = scratch[...].astype(jnp.bfloat16)


def pack(old_codes, n_fsdp):
    rows, width = old_codes.shape
    packed_rows = rows * width // n_fsdp // TILE
    sections = n_fsdp // PACK_STEPS
    return pl.pallas_call(
        pack_kernel,
        out_shape=jax.ShapeDtypeStruct((n_fsdp, packed_rows, TILE), jnp.bfloat16),
        grid=(PACK_STEPS,),
        in_specs=[pl.BlockSpec((rows, width // PACK_STEPS), lambda i: (0, i))],
        out_specs=pl.BlockSpec((sections, packed_rows, TILE), lambda i: (i, 0, 0)),
        scratch_shapes=[pltpu.VMEM((packed_rows, TILE), jnp.float32)],
        name="pack",
    )(old_codes)


def requantize_kernel(scale_ref, in_ref, codes_ref, weight_ref, new_scale_ref, rows_ref, piece_ref):
    *senders, packed_rows, _ = in_ref.shape
    n_x, n_c, parts, n_l = senders
    total_rows, width = rows_ref.shape
    tiles = width // TILE
    rows = packed_rows // tiles

    for x, core, part, low in itertools.product(*map(range, senders)):
        piece_ref[core] = in_ref[x, core, part, low].astype(jnp.float32)
        base = (((part * n_x + x) * n_l + low) * n_c + core) * rows
        for tile in range(tiles):
            rows_ref[pl.ds(base, rows), tile * TILE : (tile + 1) * TILE] = piece_ref[
                core, pl.ds(tile * rows, rows), :
            ]
    lane = lax.broadcasted_iota(jnp.int32, (1, TILE), 1)

    def one_row(row, carry):
        at = pl.ds(pl.multiple_of(row * TILE, TILE), TILE)
        line = jnp.zeros((1, TILE), jnp.float32)
        for tile in range(tiles):
            cols = slice(tile * TILE, (tile + 1) * TILE)
            codes = rows_ref[at, cols]
            scale = scale_ref[row, tile]
            top = jnp.max(jnp.abs(codes), axis=0, keepdims=True)
            new_scale = jnp.max(top, axis=1, keepdims=True) * scale + EPSILON
            line = jnp.where(lane == tile, new_scale, line)
            new_codes = (codes * scale / new_scale).astype(jnp.bfloat16)
            codes_ref[at, cols] = new_codes
            weight_ref[at, cols] = (new_codes.astype(jnp.float32) * new_scale).astype(jnp.bfloat16)
        new_scale_ref[pl.ds(row, 1), :] = line
        return carry

    lax.fori_loop(0, total_rows // TILE, one_row, 0)


def requantize(moved, scale_block, width):
    *senders, packed_rows, _ = moved.shape
    total_rows = math.prod(senders) * packed_rows * TILE // width
    vmem = pl.BlockSpec(memory_space=pltpu.VMEM)
    return pl.pallas_call(
        requantize_kernel,
        out_shape=(
            jax.ShapeDtypeStruct((total_rows, width), jnp.bfloat16),
            jax.ShapeDtypeStruct((total_rows, width), jnp.bfloat16),
            jax.ShapeDtypeStruct((total_rows // TILE, TILE), jnp.float32),
        ),
        in_specs=[pl.BlockSpec(memory_space=pltpu.SMEM), vmem],
        out_specs=(vmem, vmem, vmem),
        scratch_shapes=[
            pltpu.VMEM((total_rows, width), jnp.float32),
            pltpu.VMEM((2, packed_rows, TILE), jnp.float32),
        ],
        compiler_params=pltpu.CompilerParams(vmem_limit_bytes=20 << 20),
        name="requantize",
    )(scale_block, moved)


def half_product_kernel(parity_ref, even_ref, odd_ref, weight_ref, out_ref):
    tokens = jnp.concatenate([even_ref[...], odd_ref[...]], axis=0)
    out_ref[...] = jnp.dot(
        tokens, weight_ref[...], preferred_element_type=jnp.float32
    ).astype(jnp.bfloat16)


def half_product(every, weight, parity, owners):
    depth, width = weight.shape
    rows = every.shape[0] // owners
    count = every.shape[0] // 2
    return pl.pallas_call(
        half_product_kernel,
        out_shape=jax.ShapeDtypeStruct((count, width), jnp.bfloat16),
        grid_spec=pltpu.PrefetchScalarGridSpec(
            num_scalar_prefetch=1,
            grid=(owners // 4,),
            in_specs=[
                pl.BlockSpec((rows, depth), lambda i, parity: (4 * i + parity[0], 0)),
                pl.BlockSpec((rows, depth), lambda i, parity: (4 * i + 2 + parity[0], 0)),
                pl.BlockSpec((depth, width), lambda i, parity: (0, 0), pipeline_mode=pl.Buffered(1)),
            ],
            out_specs=pl.BlockSpec((2 * rows, width), lambda i, parity: (i, 0)),
        ),
        compiler_params=pltpu.CompilerParams(vmem_limit_bytes=56 << 20),
        cost_estimate=pl.CostEstimate(
            flops=2 * count * depth * width,
            bytes_accessed=2 * (count * depth + depth * width + count * width),
            transcendentals=0,
        ),
        name="half_product",
    )(parity, every, every, weight)


def body(old_codes, old_scales, gate_pre, up_pre):
    n_fsdp = lax.axis_size(FSDP)
    n_tensor = lax.axis_size(TENSOR)
    f_index = lax.axis_index(FSDP)
    t_index = lax.axis_index(TENSOR)
    block_rows, full_width = old_codes.shape
    col_width = full_width // n_fsdp
    col_tiles = col_width // TILE
    per_owner = n_fsdp // n_tensor
    own_rows = block_rows * n_fsdp
    row_tiles = own_rows // TILE
    hidden = (jax.nn.silu(gate_pre.astype(jnp.float32)) * up_pre.astype(jnp.float32)).astype(
        jnp.bfloat16
    )
    n_z = lax.axis_size("z")
    n_h = lax.axis_size("h")
    near = lax.all_gather(hidden, "h", axis=0, tiled=True)
    packed = pack(old_codes, n_fsdp)
    packed_rows = packed.shape[1]

    def reordered(sections, sizes, order):
        parted = sections.reshape(*sizes, packed_rows, TILE)
        return parted.transpose(*order, 4, 5).reshape(n_fsdp, packed_rows, TILE)

    n_x, n_l, n_c = (lax.axis_size(name) for name in TENSOR)
    along_z = lax.all_to_all(packed, "z", split_axis=0, concat_axis=0, tiled=True)
    near, along_z = lax.optimization_barrier((near, along_z))
    every = lax.all_gather(near, "z", axis=0, tiled=True)
    by_column = reordered(along_z, (1, n_z // n_l, n_l, n_h), (0, 3, 2, 1))
    along_y = lax.all_to_all(by_column, ("h", "l"), split_axis=0, concat_axis=0, tiled=True)
    by_owner = reordered(along_y, (n_c, n_h // n_c, n_l, n_z // n_l), (3, 0, 1, 2))
    moved = lax.all_to_all(by_owner, ("x", "c"), split_axis=0, concat_axis=0, tiled=True)
    scale_block = lax.dynamic_slice(
        old_scales, (t_index * row_tiles, f_index * col_tiles), (row_tiles, col_tiles)
    )
    new_codes, weight, new_scale = requantize(
        moved.reshape(n_x, n_c, per_owner, n_l, packed_rows, TILE), scale_block, col_width
    )
    codes_t = new_codes.T
    scales_t = new_scale[:, :col_tiles].T

    core = lax.axis_index("c").astype(jnp.int32).reshape(1)
    other = half_product(every, weight, 1 - core, n_tensor)
    other = lax.ppermute(other, "c", [(0, 1), (1, 0)])
    own = half_product(every, weight, core, n_tensor)
    share = (own.astype(jnp.float32) + other.astype(jnp.float32)).astype(jnp.bfloat16)
    shares = lax.all_to_all(share, ("x", "l"), split_axis=0, concat_axis=0, tiled=True)
    mixed = jnp.sum(
        shares.reshape(n_tensor // n_c, -1, col_width).astype(jnp.float32), axis=0
    ).astype(jnp.bfloat16)
    return (mixed, codes_t, scales_t)


def solution(mesh):
    fine = Mesh(mesh.devices.reshape(SIZES), AXES)
    return jax.shard_map(
        body,
        mesh=fine,
        in_specs=(P(FSDP + TENSOR, None), P(), P(FSDP, TENSOR), P(FSDP, TENSOR)),
        out_specs=(P(TENSOR, FSDP), P(FSDP, TENSOR), P(FSDP, TENSOR)),
        check_vma=False,
    )
```

```python
import jax
import jax.numpy as jnp
from jax import lax
from jax.experimental import pallas as pl
from jax.experimental.pallas import tpu as pltpu
from jax.sharding import Mesh, PartitionSpec as P

TILE = 128
EPSILON = 1e-06
AXES = ("z", "h", "x", "l", "c")
SIZES = (8, 4, 4, 2, 2)
FSDP = ("z", "h")
TENSOR = ("x", "l", "c")
PACK_STEPS = 4


def pack_kernel(in_ref, *refs):
    *out_refs, scratch = refs
    rows = in_ref.shape[0]
    sections, packed_rows, lanes = out_refs[0].shape
    tiles = packed_rows // rows
    for section in range(sections):
        for which, out_ref in enumerate(out_refs):
            for tile in range(tiles):
                at = ((section * len(out_refs) + which) * tiles + tile) * lanes
                scratch[which, pl.ds(tile * rows, rows), :] = in_ref[:, pl.ds(at, lanes)].astype(
                    jnp.float32
                )
            out_ref[section] = scratch[which].astype(jnp.bfloat16)


def pack(old_codes, n_fsdp, parts):
    rows, width = old_codes.shape
    packed_rows = rows * width // n_fsdp // TILE // parts
    sections = n_fsdp // PACK_STEPS
    shape = jax.ShapeDtypeStruct((n_fsdp, packed_rows, TILE), jnp.bfloat16)
    block = pl.BlockSpec((sections, packed_rows, TILE), lambda i: (i, 0, 0))
    return pl.pallas_call(
        pack_kernel,
        out_shape=(shape,) * parts,
        grid=(PACK_STEPS,),
        in_specs=[pl.BlockSpec((rows, width // PACK_STEPS), lambda i: (0, i))],
        out_specs=(block,) * parts,
        scratch_shapes=[pltpu.VMEM((parts, packed_rows, TILE), jnp.float32)],
        compiler_params=pltpu.CompilerParams(vmem_limit_bytes=12 << 20),
        name="pack",
    )(old_codes)


def requantize_kernel(scale_ref, in_ref, codes_ref, weight_ref, new_scale_ref, rows_ref, piece_ref):
    senders, parts, packed_rows, _ = in_ref.shape
    total_rows, width = rows_ref.shape
    tiles = width // TILE
    rows = packed_rows // tiles

    for part in range(parts):
        for sender in range(senders):
            slot = sender % 2
            piece_ref[slot] = in_ref[sender, part].astype(jnp.float32)
            base = (part * senders + sender) * rows
            for tile in range(tiles):
                rows_ref[pl.ds(base, rows), tile * TILE : (tile + 1) * TILE] = piece_ref[
                    slot, pl.ds(tile * rows, rows), :
                ]
    lane = lax.broadcasted_iota(jnp.int32, (1, TILE), 1)

    def one_row(row, carry):
        at = pl.ds(pl.multiple_of(row * TILE, TILE), TILE)
        line = jnp.zeros((1, TILE), jnp.float32)
        for tile in range(tiles):
            cols = slice(tile * TILE, (tile + 1) * TILE)
            codes = rows_ref[at, cols]
            scale = scale_ref[row, tile]
            top = jnp.max(jnp.abs(codes), axis=0, keepdims=True)
            new_scale = jnp.max(top, axis=1, keepdims=True) * scale + EPSILON
            line = jnp.where(lane == tile, new_scale, line)
            new_codes = (codes * scale / new_scale).astype(jnp.bfloat16)
            codes_ref[at, cols] = new_codes
            weight_ref[at, cols] = (new_codes.astype(jnp.float32) * new_scale).astype(jnp.bfloat16)
        new_scale_ref[pl.ds(row, 1), :] = line
        return carry

    lax.fori_loop(0, total_rows // TILE, one_row, 0)


def requantize(moved, scale_block, width):
    senders, parts, packed_rows, _ = moved.shape
    total_rows = senders * parts * packed_rows * TILE // width
    vmem = pl.BlockSpec(memory_space=pltpu.VMEM)
    return pl.pallas_call(
        requantize_kernel,
        out_shape=(
            jax.ShapeDtypeStruct((total_rows, width), jnp.bfloat16),
            jax.ShapeDtypeStruct((total_rows, width), jnp.bfloat16),
            jax.ShapeDtypeStruct((total_rows // TILE, TILE), jnp.float32),
        ),
        in_specs=[pl.BlockSpec(memory_space=pltpu.SMEM), vmem],
        out_specs=(vmem, vmem, vmem),
        scratch_shapes=[
            pltpu.VMEM((total_rows, width), jnp.float32),
            pltpu.VMEM((2, packed_rows, TILE), jnp.float32),
        ],
        compiler_params=pltpu.CompilerParams(vmem_limit_bytes=20 << 20),
        name="requantize",
    )(scale_block, moved)


def body(old_codes, old_scales, gate_pre, up_pre):
    n_fsdp = lax.axis_size(FSDP)
    n_tensor = lax.axis_size(TENSOR)
    f_index = lax.axis_index(FSDP)
    t_index = lax.axis_index(TENSOR)
    block_rows, full_width = old_codes.shape
    col_width = full_width // n_fsdp
    col_tiles = col_width // TILE
    per_owner = n_fsdp // n_tensor
    own_rows = block_rows * n_fsdp
    row_tiles = own_rows // TILE
    hidden = (jax.nn.silu(gate_pre.astype(jnp.float32)) * up_pre.astype(jnp.float32)).astype(
        jnp.bfloat16
    )
    n_z = lax.axis_size("z")
    n_h = lax.axis_size("h")
    near = lax.all_gather(hidden, "h", axis=0, tiled=True)
    staged, direct = pack(old_codes, n_fsdp, 2)
    part_rows = staged.shape[1]
    packed_rows = 2 * part_rows

    def swapped(sections, rows):
        return jnp.swapaxes(sections.reshape(rows, -1, part_rows, TILE), 0, 1).reshape(
            n_fsdp, part_rows, TILE
        )

    along_z = lax.all_to_all(staged, "z", split_axis=0, concat_axis=0, tiled=True)
    near, along_z = lax.optimization_barrier((near, along_z))
    every = lax.all_gather(near, "z", axis=0, tiled=True)
    staged = lax.all_to_all(swapped(along_z, n_z), "h", split_axis=0, concat_axis=0, tiled=True)
    staged, direct = lax.optimization_barrier((staged, direct))
    direct = lax.all_to_all(direct, FSDP, split_axis=0, concat_axis=0, tiled=True)
    sectioned = jnp.concatenate([swapped(staged, n_h), direct], axis=1)
    moved = lax.all_to_all(
        sectioned.reshape(n_tensor, per_owner * packed_rows, TILE),
        TENSOR,
        split_axis=0,
        concat_axis=0,
        tiled=True,
    )
    scale_block = lax.dynamic_slice(
        old_scales, (t_index * row_tiles, f_index * col_tiles), (row_tiles, col_tiles)
    )
    new_codes, weight, new_scale = requantize(
        moved.reshape(n_tensor, per_owner, packed_rows, TILE), scale_block, col_width
    )
    codes_t = new_codes.T
    scales_t = new_scale[:, :col_tiles].T

    n_c = lax.axis_size("c")
    core = lax.axis_index("c")
    share = jnp.dot(every, weight, preferred_element_type=jnp.float32).astype(jnp.bfloat16)
    by_core = share.reshape(n_tensor // n_c, n_c, -1, col_width)
    other = lax.dynamic_index_in_dim(by_core, 1 - core, 1, keepdims=False)
    other = lax.ppermute(other, "c", [(0, 1), (1, 0)])
    own = lax.dynamic_index_in_dim(by_core, core, 1, keepdims=False)
    share = (own.astype(jnp.float32) + other.astype(jnp.float32)).astype(jnp.bfloat16)
    shares = lax.all_to_all(share, ("x", "l"), split_axis=0, concat_axis=0, tiled=True)
    mixed = jnp.sum(
        shares.reshape(n_tensor // n_c, -1, col_width).astype(jnp.float32), axis=0
    ).astype(jnp.bfloat16)
    return (mixed, codes_t, scales_t)


def solution(mesh):
    fine = Mesh(mesh.devices.reshape(SIZES), AXES)
    return jax.shard_map(
        body,
        mesh=fine,
        in_specs=(P(FSDP + TENSOR, None), P(), P(FSDP, TENSOR), P(FSDP, TENSOR)),
        out_specs=(P(TENSOR, FSDP), P(FSDP, TENSOR), P(FSDP, TENSOR)),
        check_vma=False,
    )
```

```python
import jax
import jax.numpy as jnp
from jax import lax
from jax.experimental import pallas as pl
from jax.experimental.pallas import tpu as pltpu
from jax.sharding import Mesh, PartitionSpec as P

TILE = 128
EPSILON = 1e-06
AXES = ("z", "h", "x", "l", "c")
SIZES = (8, 4, 4, 2, 2)
FSDP = ("z", "h")
TENSOR = ("x", "l", "c")
PACK_STEPS = 4


def pack_kernel(in_ref, *refs):
    *out_refs, scratch = refs
    rows = in_ref.shape[0]
    sections, packed_rows, lanes = out_refs[0].shape
    tiles = packed_rows // rows
    for section in range(sections):
        for which, out_ref in enumerate(out_refs):
            for tile in range(tiles):
                at = ((section * len(out_refs) + which) * tiles + tile) * lanes
                scratch[which, pl.ds(tile * rows, rows), :] = in_ref[:, pl.ds(at, lanes)].astype(
                    jnp.float32
                )
            out_ref[section] = scratch[which].astype(jnp.bfloat16)


def pack(old_codes, n_fsdp, parts):
    rows, width = old_codes.shape
    packed_rows = rows * width // n_fsdp // TILE // parts
    sections = n_fsdp // PACK_STEPS
    shape = jax.ShapeDtypeStruct((n_fsdp, packed_rows, TILE), jnp.bfloat16)
    block = pl.BlockSpec((sections, packed_rows, TILE), lambda i: (i, 0, 0))
    return pl.pallas_call(
        pack_kernel,
        out_shape=(shape,) * parts,
        grid=(PACK_STEPS,),
        in_specs=[pl.BlockSpec((rows, width // PACK_STEPS), lambda i: (0, i))],
        out_specs=(block,) * parts,
        scratch_shapes=[pltpu.VMEM((parts, packed_rows, TILE), jnp.float32)],
        compiler_params=pltpu.CompilerParams(vmem_limit_bytes=12 << 20),
        name="pack",
    )(old_codes)


def requantize_kernel(scale_ref, in_ref, codes_ref, weight_ref, new_scale_ref, rows_ref, piece_ref):
    senders, parts, packed_rows, _ = in_ref.shape
    total_rows, width = rows_ref.shape
    tiles = width // TILE
    rows = packed_rows // tiles

    for part in range(parts):
        for sender in range(senders):
            slot = sender % 2
            piece_ref[slot] = in_ref[sender, part].astype(jnp.float32)
            base = (part * senders + sender) * rows
            for tile in range(tiles):
                rows_ref[pl.ds(base, rows), tile * TILE : (tile + 1) * TILE] = piece_ref[
                    slot, pl.ds(tile * rows, rows), :
                ]
    lane = lax.broadcasted_iota(jnp.int32, (1, TILE), 1)

    def one_row(row, carry):
        at = pl.ds(pl.multiple_of(row * TILE, TILE), TILE)
        line = jnp.zeros((1, TILE), jnp.float32)
        for tile in range(tiles):
            cols = slice(tile * TILE, (tile + 1) * TILE)
            codes = rows_ref[at, cols]
            scale = scale_ref[row, tile]
            top = jnp.max(jnp.abs(codes), axis=0, keepdims=True)
            new_scale = jnp.max(top, axis=1, keepdims=True) * scale + EPSILON
            line = jnp.where(lane == tile, new_scale, line)
            new_codes = (codes * scale / new_scale).astype(jnp.bfloat16)
            codes_ref[at, cols] = new_codes
            weight_ref[at, cols] = (new_codes.astype(jnp.float32) * new_scale).astype(jnp.bfloat16)
        new_scale_ref[pl.ds(row, 1), :] = line
        return carry

    lax.fori_loop(0, total_rows // TILE, one_row, 0)


def requantize(moved, scale_block, width):
    senders, parts, packed_rows, _ = moved.shape
    total_rows = senders * parts * packed_rows * TILE // width
    vmem = pl.BlockSpec(memory_space=pltpu.VMEM)
    return pl.pallas_call(
        requantize_kernel,
        out_shape=(
            jax.ShapeDtypeStruct((total_rows, width), jnp.bfloat16),
            jax.ShapeDtypeStruct((total_rows, width), jnp.bfloat16),
            jax.ShapeDtypeStruct((total_rows // TILE, TILE), jnp.float32),
        ),
        in_specs=[pl.BlockSpec(memory_space=pltpu.SMEM), vmem],
        out_specs=(vmem, vmem, vmem),
        scratch_shapes=[
            pltpu.VMEM((total_rows, width), jnp.float32),
            pltpu.VMEM((2, packed_rows, TILE), jnp.float32),
        ],
        compiler_params=pltpu.CompilerParams(vmem_limit_bytes=20 << 20),
        name="requantize",
    )(scale_block, moved)


def half_product_kernel(parity_ref, even_ref, odd_ref, weight_ref, out_ref):
    tokens = jnp.concatenate([even_ref[...], odd_ref[...]], axis=0)
    out_ref[...] = jnp.dot(
        tokens, weight_ref[...], preferred_element_type=jnp.float32
    ).astype(jnp.bfloat16)


def half_product(every, weight, parity, owners):
    depth, width = weight.shape
    rows = every.shape[0] // owners
    count = every.shape[0] // 2
    return pl.pallas_call(
        half_product_kernel,
        out_shape=jax.ShapeDtypeStruct((count, width), jnp.bfloat16),
        grid_spec=pltpu.PrefetchScalarGridSpec(
            num_scalar_prefetch=1,
            grid=(owners // 4,),
            in_specs=[
                pl.BlockSpec((rows, depth), lambda i, parity: (4 * i + parity[0], 0)),
                pl.BlockSpec((rows, depth), lambda i, parity: (4 * i + 2 + parity[0], 0)),
                pl.BlockSpec(memory_space=pltpu.VMEM),
            ],
            out_specs=pl.BlockSpec((2 * rows, width), lambda i, parity: (i, 0)),
        ),
        compiler_params=pltpu.CompilerParams(vmem_limit_bytes=10 << 20),
        cost_estimate=pl.CostEstimate(
            flops=2 * count * depth * width,
            bytes_accessed=2 * (count * depth + depth * width + count * width),
            transcendentals=0,
        ),
        name="half_product",
    )(parity, every, every, weight)


def body(old_codes, old_scales, gate_pre, up_pre):
    n_fsdp = lax.axis_size(FSDP)
    n_tensor = lax.axis_size(TENSOR)
    f_index = lax.axis_index(FSDP)
    t_index = lax.axis_index(TENSOR)
    block_rows, full_width = old_codes.shape
    col_width = full_width // n_fsdp
    col_tiles = col_width // TILE
    per_owner = n_fsdp // n_tensor
    own_rows = block_rows * n_fsdp
    row_tiles = own_rows // TILE
    hidden = (jax.nn.silu(gate_pre.astype(jnp.float32)) * up_pre.astype(jnp.float32)).astype(
        jnp.bfloat16
    )
    n_z = lax.axis_size("z")
    n_h = lax.axis_size("h")
    near = lax.all_gather(hidden, "h", axis=0, tiled=True)
    staged, direct = pack(old_codes, n_fsdp, 2)
    part_rows = staged.shape[1]
    packed_rows = 2 * part_rows

    def swapped(sections, rows):
        return jnp.swapaxes(sections.reshape(rows, -1, part_rows, TILE), 0, 1).reshape(
            n_fsdp, part_rows, TILE
        )

    along_z = lax.all_to_all(staged, "z", split_axis=0, concat_axis=0, tiled=True)
    near, along_z = lax.optimization_barrier((near, along_z))
    every = lax.all_gather(near, "z", axis=0, tiled=True)
    staged = lax.all_to_all(swapped(along_z, n_z), "h", split_axis=0, concat_axis=0, tiled=True)
    staged, direct = lax.optimization_barrier((staged, direct))
    direct = lax.all_to_all(direct, FSDP, split_axis=0, concat_axis=0, tiled=True)
    sectioned = jnp.concatenate([swapped(staged, n_h), direct], axis=1)
    moved = lax.all_to_all(
        sectioned.reshape(n_tensor, per_owner * packed_rows, TILE),
        TENSOR,
        split_axis=0,
        concat_axis=0,
        tiled=True,
    )
    scale_block = lax.dynamic_slice(
        old_scales, (t_index * row_tiles, f_index * col_tiles), (row_tiles, col_tiles)
    )
    new_codes, weight, new_scale = requantize(
        moved.reshape(n_tensor, per_owner, packed_rows, TILE), scale_block, col_width
    )
    codes_t = new_codes.T
    scales_t = new_scale[:, :col_tiles].T

    n_c = lax.axis_size("c")
    core = lax.axis_index("c").astype(jnp.int32).reshape(1)
    every = pltpu.with_memory_space_constraint(every, pltpu.HBM)
    other = half_product(every, weight, 1 - core, n_tensor)
    other = lax.ppermute(other, "c", [(0, 1), (1, 0)])
    own = half_product(every, weight, core, n_tensor)
    share = (own.astype(jnp.float32) + other.astype(jnp.float32)).astype(jnp.bfloat16)
    shares = lax.all_to_all(share, ("x", "l"), split_axis=0, concat_axis=0, tiled=True)
    mixed = jnp.sum(
        shares.reshape(n_tensor // n_c, -1, col_width).astype(jnp.float32), axis=0
    ).astype(jnp.bfloat16)
    return (mixed, codes_t, scales_t)


def solution(mesh):
    fine = Mesh(mesh.devices.reshape(SIZES), AXES)
    return jax.shard_map(
        body,
        mesh=fine,
        in_specs=(P(FSDP + TENSOR, None), P(), P(FSDP, TENSOR), P(FSDP, TENSOR)),
        out_specs=(P(TENSOR, FSDP), P(FSDP, TENSOR), P(FSDP, TENSOR)),
        check_vma=False,
    )
```

```python
import jax
import jax.numpy as jnp
from jax import lax
from jax.experimental import pallas as pl
from jax.experimental.pallas import tpu as pltpu
from jax.sharding import Mesh, PartitionSpec as P

TILE = 128
EPSILON = 1e-06
AXES = ("z", "h", "x", "l", "c")
SIZES = (8, 4, 4, 2, 2)
FSDP = ("z", "h")
TENSOR = ("x", "l", "c")
PACK_STEPS = 8


def pack_kernel(in_ref, *refs):
    *out_refs, scratch = refs
    rows = in_ref.shape[0]
    sections, packed_rows, lanes = out_refs[0].shape
    tiles = packed_rows // rows
    for section in range(sections):
        for which, out_ref in enumerate(out_refs):
            for tile in range(tiles):
                at = ((section * len(out_refs) + which) * tiles + tile) * lanes
                scratch[which, pl.ds(tile * rows, rows), :] = in_ref[:, pl.ds(at, lanes)].astype(
                    jnp.float32
                )
            out_ref[section] = scratch[which].astype(jnp.bfloat16)


def pack(old_codes, n_fsdp, parts):
    rows, width = old_codes.shape
    packed_rows = rows * width // n_fsdp // TILE // parts
    sections = n_fsdp // PACK_STEPS
    shape = jax.ShapeDtypeStruct((n_fsdp, packed_rows, TILE), jnp.bfloat16)
    block = pl.BlockSpec((sections, packed_rows, TILE), lambda i: (i, 0, 0))
    return pl.pallas_call(
        pack_kernel,
        out_shape=(shape,) * parts,
        grid=(PACK_STEPS,),
        in_specs=[pl.BlockSpec((rows, width // PACK_STEPS), lambda i: (0, i))],
        out_specs=(block,) * parts,
        scratch_shapes=[pltpu.VMEM((parts, packed_rows, TILE), jnp.float32)],
        name="pack",
    )(old_codes)


def requantize_kernel(scale_ref, in_ref, codes_ref, weight_ref, new_scale_ref, rows_ref, piece_ref):
    senders, parts, packed_rows, _ = in_ref.shape
    total_rows, width = rows_ref.shape
    tiles = width // TILE
    rows = packed_rows // tiles

    for part in range(parts):
        for sender in range(senders):
            slot = sender % 2
            piece_ref[slot] = in_ref[sender, part].astype(jnp.float32)
            base = (part * senders + sender) * rows
            for tile in range(tiles):
                rows_ref[pl.ds(base, rows), tile * TILE : (tile + 1) * TILE] = piece_ref[
                    slot, pl.ds(tile * rows, rows), :
                ]
    lane = lax.broadcasted_iota(jnp.int32, (1, TILE), 1)

    def one_row(row, carry):
        at = pl.ds(pl.multiple_of(row * TILE, TILE), TILE)
        line = jnp.zeros((1, TILE), jnp.float32)
        for tile in range(tiles):
            cols = slice(tile * TILE, (tile + 1) * TILE)
            codes = rows_ref[at, cols]
            scale = scale_ref[row, tile]
            top = jnp.max(jnp.abs(codes), axis=0, keepdims=True)
            new_scale = jnp.max(top, axis=1, keepdims=True) * scale + EPSILON
            line = jnp.where(lane == tile, new_scale, line)
            new_codes = (codes * scale / new_scale).astype(jnp.bfloat16)
            codes_ref[at, cols] = new_codes
            weight_ref[at, cols] = (new_codes.astype(jnp.float32) * new_scale).astype(jnp.bfloat16)
        new_scale_ref[pl.ds(row, 1), :] = line
        return carry

    lax.fori_loop(0, total_rows // TILE, one_row, 0)


def requantize(moved, scale_block, width):
    senders, parts, packed_rows, _ = moved.shape
    total_rows = senders * parts * packed_rows * TILE // width
    vmem = pl.BlockSpec(memory_space=pltpu.VMEM)
    return pl.pallas_call(
        requantize_kernel,
        out_shape=(
            jax.ShapeDtypeStruct((total_rows, width), jnp.bfloat16),
            jax.ShapeDtypeStruct((total_rows, width), jnp.bfloat16),
            jax.ShapeDtypeStruct((total_rows // TILE, TILE), jnp.float32),
        ),
        in_specs=[pl.BlockSpec(memory_space=pltpu.SMEM), vmem],
        out_specs=(vmem, vmem, vmem),
        scratch_shapes=[
            pltpu.VMEM((total_rows, width), jnp.float32),
            pltpu.VMEM((2, packed_rows, TILE), jnp.float32),
        ],
        compiler_params=pltpu.CompilerParams(vmem_limit_bytes=20 << 20),
        name="requantize",
    )(scale_block, moved)


def half_product_kernel(parity_ref, even_ref, odd_ref, weight_ref, out_ref):
    tokens = jnp.concatenate([even_ref[...], odd_ref[...]], axis=0)
    out_ref[...] = jnp.dot(
        tokens, weight_ref[...], preferred_element_type=jnp.float32
    ).astype(jnp.bfloat16)


def half_product(every, weight, parity, owners):
    depth, width = weight.shape
    rows = every.shape[0] // owners
    count = every.shape[0] // 2
    return pl.pallas_call(
        half_product_kernel,
        out_shape=jax.ShapeDtypeStruct((count, width), jnp.bfloat16),
        grid_spec=pltpu.PrefetchScalarGridSpec(
            num_scalar_prefetch=1,
            grid=(owners // 4,),
            in_specs=[
                pl.BlockSpec((rows, depth), lambda i, parity: (4 * i + parity[0], 0)),
                pl.BlockSpec((rows, depth), lambda i, parity: (4 * i + 2 + parity[0], 0)),
                pl.BlockSpec(memory_space=pltpu.VMEM),
            ],
            out_specs=pl.BlockSpec((2 * rows, width), lambda i, parity: (i, 0)),
        ),
        compiler_params=pltpu.CompilerParams(vmem_limit_bytes=10 << 20),
        cost_estimate=pl.CostEstimate(
            flops=2 * count * depth * width,
            bytes_accessed=2 * (count * depth + depth * width + count * width),
            transcendentals=0,
        ),
        name="half_product",
    )(parity, every, every, weight)


def body(old_codes, old_scales, gate_pre, up_pre):
    n_fsdp = lax.axis_size(FSDP)
    n_tensor = lax.axis_size(TENSOR)
    f_index = lax.axis_index(FSDP)
    t_index = lax.axis_index(TENSOR)
    block_rows, full_width = old_codes.shape
    col_width = full_width // n_fsdp
    col_tiles = col_width // TILE
    per_owner = n_fsdp // n_tensor
    own_rows = block_rows * n_fsdp
    row_tiles = own_rows // TILE
    hidden = (jax.nn.silu(gate_pre.astype(jnp.float32)) * up_pre.astype(jnp.float32)).astype(
        jnp.bfloat16
    )
    n_z = lax.axis_size("z")
    n_h = lax.axis_size("h")
    near = lax.all_gather(hidden, "h", axis=0, tiled=True)
    staged, direct = pack(old_codes, n_fsdp, 2)
    part_rows = staged.shape[1]
    packed_rows = 2 * part_rows

    def swapped(sections, rows):
        return jnp.swapaxes(sections.reshape(rows, -1, part_rows, TILE), 0, 1).reshape(
            n_fsdp, part_rows, TILE
        )

    along_z = lax.all_to_all(staged, "z", split_axis=0, concat_axis=0, tiled=True)
    near, along_z = lax.optimization_barrier((near, along_z))
    every = lax.all_gather(near, "z", axis=0, tiled=True)
    staged = lax.all_to_all(swapped(along_z, n_z), "h", split_axis=0, concat_axis=0, tiled=True)
    staged, direct = lax.optimization_barrier((staged, direct))
    direct = lax.all_to_all(direct, FSDP, split_axis=0, concat_axis=0, tiled=True)
    sectioned = jnp.concatenate([swapped(staged, n_h), direct], axis=1)
    moved = lax.all_to_all(
        sectioned.reshape(n_tensor, per_owner * packed_rows, TILE),
        TENSOR,
        split_axis=0,
        concat_axis=0,
        tiled=True,
    )
    scale_block = lax.dynamic_slice(
        old_scales, (t_index * row_tiles, f_index * col_tiles), (row_tiles, col_tiles)
    )
    new_codes, weight, new_scale = requantize(
        moved.reshape(n_tensor, per_owner, packed_rows, TILE), scale_block, col_width
    )
    codes_t = new_codes.T
    scales_t = new_scale[:, :col_tiles].T

    n_c = lax.axis_size("c")
    core = lax.axis_index("c").astype(jnp.int32).reshape(1)
    every = pltpu.with_memory_space_constraint(every, pltpu.HBM)
    other = half_product(every, weight, 1 - core, n_tensor)
    other = lax.ppermute(other, "c", [(0, 1), (1, 0)])
    own = half_product(every, weight, core, n_tensor)
    share = (own.astype(jnp.float32) + other.astype(jnp.float32)).astype(jnp.bfloat16)
    shares = lax.all_to_all(share, ("x", "l"), split_axis=0, concat_axis=0, tiled=True)
    mixed = jnp.sum(
        shares.reshape(n_tensor // n_c, -1, col_width).astype(jnp.float32), axis=0
    ).astype(jnp.bfloat16)
    return (mixed, codes_t, scales_t)


def solution(mesh):
    fine = Mesh(mesh.devices.reshape(SIZES), AXES)
    return jax.shard_map(
        body,
        mesh=fine,
        in_specs=(P(FSDP + TENSOR, None), P(), P(FSDP, TENSOR), P(FSDP, TENSOR)),
        out_specs=(P(TENSOR, FSDP), P(FSDP, TENSOR), P(FSDP, TENSOR)),
        check_vma=False,
    )
```

```python
import jax
import jax.numpy as jnp
from jax import lax
from jax.experimental import pallas as pl
from jax.experimental.pallas import tpu as pltpu
from jax.sharding import Mesh, PartitionSpec as P

TILE = 128
EPSILON = 1e-06
AXES = ("z", "h", "x", "l", "c")
SIZES = (8, 4, 4, 2, 2)
FSDP = ("z", "h")
TENSOR = ("x", "l", "c")
PACK_STEPS = 2


def pack_kernel(in_ref, *refs):
    *out_refs, scratch = refs
    rows = in_ref.shape[0]
    sections, packed_rows, lanes = out_refs[0].shape
    tiles = packed_rows // rows
    for section in range(sections):
        for which, out_ref in enumerate(out_refs):
            for tile in range(tiles):
                at = ((section * len(out_refs) + which) * tiles + tile) * lanes
                scratch[which, pl.ds(tile * rows, rows), :] = in_ref[:, pl.ds(at, lanes)].astype(
                    jnp.float32
                )
            out_ref[section] = scratch[which].astype(jnp.bfloat16)


def pack(old_codes, n_fsdp, parts):
    rows, width = old_codes.shape
    packed_rows = rows * width // n_fsdp // TILE // parts
    sections = n_fsdp // PACK_STEPS
    shape = jax.ShapeDtypeStruct((n_fsdp, packed_rows, TILE), jnp.bfloat16)
    block = pl.BlockSpec((sections, packed_rows, TILE), lambda i: (i, 0, 0))
    return pl.pallas_call(
        pack_kernel,
        out_shape=(shape,) * parts,
        grid=(PACK_STEPS,),
        in_specs=[pl.BlockSpec((rows, width // PACK_STEPS), lambda i: (0, i))],
        out_specs=(block,) * parts,
        scratch_shapes=[pltpu.VMEM((parts, packed_rows, TILE), jnp.float32)],
        compiler_params=pltpu.CompilerParams(vmem_limit_bytes=16 << 20),
        name="pack",
    )(old_codes)


def requantize_kernel(scale_ref, in_ref, codes_ref, weight_ref, new_scale_ref, rows_ref, piece_ref):
    senders, parts, packed_rows, _ = in_ref.shape
    total_rows, width = rows_ref.shape
    tiles = width // TILE
    rows = packed_rows // tiles

    for part in range(parts):
        for sender in range(senders):
            slot = sender % 2
            piece_ref[slot] = in_ref[sender, part].astype(jnp.float32)
            base = (part * senders + sender) * rows
            for tile in range(tiles):
                rows_ref[pl.ds(base, rows), tile * TILE : (tile + 1) * TILE] = piece_ref[
                    slot, pl.ds(tile * rows, rows), :
                ]
    lane = lax.broadcasted_iota(jnp.int32, (1, TILE), 1)

    def one_row(row, carry):
        at = pl.ds(pl.multiple_of(row * TILE, TILE), TILE)
        line = jnp.zeros((1, TILE), jnp.float32)
        for tile in range(tiles):
            cols = slice(tile * TILE, (tile + 1) * TILE)
            codes = rows_ref[at, cols]
            scale = scale_ref[row, tile]
            top = jnp.max(jnp.abs(codes), axis=0, keepdims=True)
            new_scale = jnp.max(top, axis=1, keepdims=True) * scale + EPSILON
            line = jnp.where(lane == tile, new_scale, line)
            new_codes = (codes * scale / new_scale).astype(jnp.bfloat16)
            codes_ref[at, cols] = new_codes
            weight_ref[at, cols] = (new_codes.astype(jnp.float32) * new_scale).astype(jnp.bfloat16)
        new_scale_ref[pl.ds(row, 1), :] = line
        return carry

    lax.fori_loop(0, total_rows // TILE, one_row, 0)


def requantize(moved, scale_block, width):
    senders, parts, packed_rows, _ = moved.shape
    total_rows = senders * parts * packed_rows * TILE // width
    vmem = pl.BlockSpec(memory_space=pltpu.VMEM)
    return pl.pallas_call(
        requantize_kernel,
        out_shape=(
            jax.ShapeDtypeStruct((total_rows, width), jnp.bfloat16),
            jax.ShapeDtypeStruct((total_rows, width), jnp.bfloat16),
            jax.ShapeDtypeStruct((total_rows // TILE, TILE), jnp.float32),
        ),
        in_specs=[pl.BlockSpec(memory_space=pltpu.SMEM), vmem],
        out_specs=(vmem, vmem, vmem),
        scratch_shapes=[
            pltpu.VMEM((total_rows, width), jnp.float32),
            pltpu.VMEM((2, packed_rows, TILE), jnp.float32),
        ],
        compiler_params=pltpu.CompilerParams(vmem_limit_bytes=20 << 20),
        name="requantize",
    )(scale_block, moved)


def half_product_kernel(parity_ref, even_ref, odd_ref, weight_ref, out_ref):
    tokens = jnp.concatenate([even_ref[...], odd_ref[...]], axis=0)
    out_ref[...] = jnp.dot(
        tokens, weight_ref[...], preferred_element_type=jnp.float32
    ).astype(jnp.bfloat16)


def half_product(every, weight, parity, owners):
    depth, width = weight.shape
    rows = every.shape[0] // owners
    count = every.shape[0] // 2
    return pl.pallas_call(
        half_product_kernel,
        out_shape=jax.ShapeDtypeStruct((count, width), jnp.bfloat16),
        grid_spec=pltpu.PrefetchScalarGridSpec(
            num_scalar_prefetch=1,
            grid=(owners // 4,),
            in_specs=[
                pl.BlockSpec((rows, depth), lambda i, parity: (4 * i + parity[0], 0)),
                pl.BlockSpec((rows, depth), lambda i, parity: (4 * i + 2 + parity[0], 0)),
                pl.BlockSpec(memory_space=pltpu.VMEM),
            ],
            out_specs=pl.BlockSpec((2 * rows, width), lambda i, parity: (i, 0)),
        ),
        compiler_params=pltpu.CompilerParams(vmem_limit_bytes=10 << 20),
        cost_estimate=pl.CostEstimate(
            flops=2 * count * depth * width,
            bytes_accessed=2 * (count * depth + depth * width + count * width),
            transcendentals=0,
        ),
        name="half_product",
    )(parity, every, every, weight)


def body(old_codes, old_scales, gate_pre, up_pre):
    n_fsdp = lax.axis_size(FSDP)
    n_tensor = lax.axis_size(TENSOR)
    f_index = lax.axis_index(FSDP)
    t_index = lax.axis_index(TENSOR)
    block_rows, full_width = old_codes.shape
    col_width = full_width // n_fsdp
    col_tiles = col_width // TILE
    per_owner = n_fsdp // n_tensor
    own_rows = block_rows * n_fsdp
    row_tiles = own_rows // TILE
    hidden = (jax.nn.silu(gate_pre.astype(jnp.float32)) * up_pre.astype(jnp.float32)).astype(
        jnp.bfloat16
    )
    n_z = lax.axis_size("z")
    n_h = lax.axis_size("h")
    near = lax.all_gather(hidden, "h", axis=0, tiled=True)
    staged, direct = pack(old_codes, n_fsdp, 2)
    part_rows = staged.shape[1]
    packed_rows = 2 * part_rows

    def swapped(sections, rows):
        return jnp.swapaxes(sections.reshape(rows, -1, part_rows, TILE), 0, 1).reshape(
            n_fsdp, part_rows, TILE
        )

    along_z = lax.all_to_all(staged, "z", split_axis=0, concat_axis=0, tiled=True)
    near, along_z = lax.optimization_barrier((near, along_z))
    every = lax.all_gather(near, "z", axis=0, tiled=True)
    staged = lax.all_to_all(swapped(along_z, n_z), "h", split_axis=0, concat_axis=0, tiled=True)
    staged, direct = lax.optimization_barrier((staged, direct))
    direct = lax.all_to_all(direct, FSDP, split_axis=0, concat_axis=0, tiled=True)
    sectioned = jnp.concatenate([swapped(staged, n_h), direct], axis=1)
    moved = lax.all_to_all(
        sectioned.reshape(n_tensor, per_owner * packed_rows, TILE),
        TENSOR,
        split_axis=0,
        concat_axis=0,
        tiled=True,
    )
    scale_block = lax.dynamic_slice(
        old_scales, (t_index * row_tiles, f_index * col_tiles), (row_tiles, col_tiles)
    )
    new_codes, weight, new_scale = requantize(
        moved.reshape(n_tensor, per_owner, packed_rows, TILE), scale_block, col_width
    )
    codes_t = new_codes.T
    scales_t = new_scale[:, :col_tiles].T

    n_c = lax.axis_size("c")
    core = lax.axis_index("c").astype(jnp.int32).reshape(1)
    every = pltpu.with_memory_space_constraint(every, pltpu.HBM)
    other = half_product(every, weight, 1 - core, n_tensor)
    other = lax.ppermute(other, "c", [(0, 1), (1, 0)])
    own = half_product(every, weight, core, n_tensor)
    share = (own.astype(jnp.float32) + other.astype(jnp.float32)).astype(jnp.bfloat16)
    shares = lax.all_to_all(share, ("x", "l"), split_axis=0, concat_axis=0, tiled=True)
    mixed = jnp.sum(
        shares.reshape(n_tensor // n_c, -1, col_width).astype(jnp.float32), axis=0
    ).astype(jnp.bfloat16)
    return (mixed, codes_t, scales_t)


def solution(mesh):
    fine = Mesh(mesh.devices.reshape(SIZES), AXES)
    return jax.shard_map(
        body,
        mesh=fine,
        in_specs=(P(FSDP + TENSOR, None), P(), P(FSDP, TENSOR), P(FSDP, TENSOR)),
        out_specs=(P(TENSOR, FSDP), P(FSDP, TENSOR), P(FSDP, TENSOR)),
        check_vma=False,
    )
```

```python
import functools

import jax
import jax.numpy as jnp
from jax import lax
from jax.experimental import pallas as pl
from jax.experimental.pallas import tpu as pltpu
from jax.sharding import Mesh, PartitionSpec as P

TILE = 128
EPSILON = 1e-06
AXES = ("z", "h", "x", "l", "c")
SIZES = (8, 4, 4, 2, 2)
FSDP = ("z", "h")
TENSOR = ("x", "l", "c")
PACK_STEPS = 2
GROUP = 4


def pack_kernel(in_ref, *refs):
    *out_refs, scratch = refs
    rows = in_ref.shape[0]
    sections, packed_rows, lanes = out_refs[0].shape
    tiles = packed_rows // rows
    for section in range(sections):
        for which, out_ref in enumerate(out_refs):
            for tile in range(tiles):
                at = ((section * len(out_refs) + which) * tiles + tile) * lanes
                scratch[which, pl.ds(tile * rows, rows), :] = in_ref[:, pl.ds(at, lanes)].astype(
                    jnp.float32
                )
            out_ref[section] = scratch[which].astype(jnp.bfloat16)


def pack(old_codes, n_fsdp, parts):
    rows, width = old_codes.shape
    packed_rows = rows * width // n_fsdp // TILE // parts
    sections = n_fsdp // PACK_STEPS
    shape = jax.ShapeDtypeStruct((n_fsdp, packed_rows, TILE), jnp.bfloat16)
    block = pl.BlockSpec((sections, packed_rows, TILE), lambda i: (i, 0, 0))
    return pl.pallas_call(
        pack_kernel,
        out_shape=(shape,) * parts,
        grid=(PACK_STEPS,),
        in_specs=[pl.BlockSpec((rows, width // PACK_STEPS), lambda i: (0, i))],
        out_specs=(block,) * parts,
        scratch_shapes=[pltpu.VMEM((parts, packed_rows, TILE), jnp.float32)],
        compiler_params=pltpu.CompilerParams(vmem_limit_bytes=16 << 20),
        name="pack",
    )(old_codes)


def requantize_kernel(scale_ref, in_ref, codes_ref, weight_ref, new_scale_ref, rows_ref, piece_ref):
    senders, parts, packed_rows, _ = in_ref.shape
    total_rows, width = rows_ref.shape
    tiles = width // TILE
    rows = packed_rows // tiles

    for part in range(parts):
        for sender in range(senders):
            slot = sender % 2
            piece_ref[slot] = in_ref[sender, part].astype(jnp.float32)
            base = (part * senders + sender) * rows
            for tile in range(tiles):
                rows_ref[pl.ds(base, rows), tile * TILE : (tile + 1) * TILE] = piece_ref[
                    slot, pl.ds(tile * rows, rows), :
                ]
    lane = lax.broadcasted_iota(jnp.int32, (1, TILE), 1)

    def one_row(row, carry):
        at = pl.ds(pl.multiple_of(row * TILE, TILE), TILE)
        line = jnp.zeros((1, TILE), jnp.float32)
        for tile in range(tiles):
            cols = slice(tile * TILE, (tile + 1) * TILE)
            codes = rows_ref[at, cols]
            scale = scale_ref[row, tile]
            top = jnp.max(jnp.abs(codes), axis=0, keepdims=True)
            new_scale = jnp.max(top, axis=1, keepdims=True) * scale + EPSILON
            line = jnp.where(lane == tile, new_scale, line)
            new_codes = (codes * scale / new_scale).astype(jnp.bfloat16)
            codes_ref[at, cols] = new_codes
            weight_ref[at, cols] = (new_codes.astype(jnp.float32) * new_scale).astype(jnp.bfloat16)
        new_scale_ref[pl.ds(row, 1), :] = line
        return carry

    lax.fori_loop(0, total_rows // TILE, one_row, 0)


def requantize(moved, scale_block, width):
    senders, parts, packed_rows, _ = moved.shape
    total_rows = senders * parts * packed_rows * TILE // width
    vmem = pl.BlockSpec(memory_space=pltpu.VMEM)
    return pl.pallas_call(
        requantize_kernel,
        out_shape=(
            jax.ShapeDtypeStruct((total_rows, width), jnp.bfloat16),
            jax.ShapeDtypeStruct((total_rows, width), jnp.bfloat16),
            jax.ShapeDtypeStruct((total_rows // TILE, TILE), jnp.float32),
        ),
        in_specs=[pl.BlockSpec(memory_space=pltpu.SMEM), vmem],
        out_specs=(vmem, vmem, vmem),
        scratch_shapes=[
            pltpu.VMEM((total_rows, width), jnp.float32),
            pltpu.VMEM((2, packed_rows, TILE), jnp.float32),
        ],
        compiler_params=pltpu.CompilerParams(vmem_limit_bytes=20 << 20),
        name="requantize",
    )(scale_block, moved)


def half_product_kernel(parity_ref, *refs):
    *token_refs, weight_ref, out_ref = refs
    tokens = jnp.concatenate([ref[...] for ref in token_refs], axis=0)
    out_ref[...] = jnp.dot(
        tokens, weight_ref[...], preferred_element_type=jnp.float32
    ).astype(jnp.bfloat16)


def owner_block(member, step, parity_ref):
    return 2 * (step * GROUP + member) + parity_ref[0], 0


def half_product(every, weight, parity, owners):
    depth, width = weight.shape
    rows = every.shape[0] // owners
    count = every.shape[0] // 2
    return pl.pallas_call(
        half_product_kernel,
        out_shape=jax.ShapeDtypeStruct((count, width), jnp.bfloat16),
        grid_spec=pltpu.PrefetchScalarGridSpec(
            num_scalar_prefetch=1,
            grid=(owners // (2 * GROUP),),
            in_specs=[
                pl.BlockSpec((rows, depth), functools.partial(owner_block, member))
                for member in range(GROUP)
            ]
            + [pl.BlockSpec(memory_space=pltpu.VMEM)],
            out_specs=pl.BlockSpec((GROUP * rows, width), lambda i, parity: (i, 0)),
        ),
        compiler_params=pltpu.CompilerParams(vmem_limit_bytes=14 << 20),
        cost_estimate=pl.CostEstimate(
            flops=2 * count * depth * width,
            bytes_accessed=2 * (count * depth + depth * width + count * width),
            transcendentals=0,
        ),
        name="half_product",
    )(parity, *(every,) * GROUP, weight)


def body(old_codes, old_scales, gate_pre, up_pre):
    n_fsdp = lax.axis_size(FSDP)
    n_tensor = lax.axis_size(TENSOR)
    f_index = lax.axis_index(FSDP)
    t_index = lax.axis_index(TENSOR)
    block_rows, full_width = old_codes.shape
    col_width = full_width // n_fsdp
    col_tiles = col_width // TILE
    per_owner = n_fsdp // n_tensor
    own_rows = block_rows * n_fsdp
    row_tiles = own_rows // TILE
    hidden = (jax.nn.silu(gate_pre.astype(jnp.float32)) * up_pre.astype(jnp.float32)).astype(
        jnp.bfloat16
    )
    n_z = lax.axis_size("z")
    n_h = lax.axis_size("h")
    near = lax.all_gather(hidden, "h", axis=0, tiled=True)
    staged, direct = pack(old_codes, n_fsdp, 2)
    part_rows = staged.shape[1]
    packed_rows = 2 * part_rows

    def swapped(sections, rows):
        return jnp.swapaxes(sections.reshape(rows, -1, part_rows, TILE), 0, 1).reshape(
            n_fsdp, part_rows, TILE
        )

    along_z = lax.all_to_all(staged, "z", split_axis=0, concat_axis=0, tiled=True)
    near, along_z = lax.optimization_barrier((near, along_z))
    every = lax.all_gather(near, "z", axis=0, tiled=True)
    staged = lax.all_to_all(swapped(along_z, n_z), "h", split_axis=0, concat_axis=0, tiled=True)
    staged, direct = lax.optimization_barrier((staged, direct))
    direct = lax.all_to_all(direct, FSDP, split_axis=0, concat_axis=0, tiled=True)
    sectioned = jnp.concatenate([swapped(staged, n_h), direct], axis=1)
    moved = lax.all_to_all(
        sectioned.reshape(n_tensor, per_owner * packed_rows, TILE),
        TENSOR,
        split_axis=0,
        concat_axis=0,
        tiled=True,
    )
    scale_block = lax.dynamic_slice(
        old_scales, (t_index * row_tiles, f_index * col_tiles), (row_tiles, col_tiles)
    )
    new_codes, weight, new_scale = requantize(
        moved.reshape(n_tensor, per_owner, packed_rows, TILE), scale_block, col_width
    )
    codes_t = new_codes.T
    scales_t = new_scale[:, :col_tiles].T

    n_c = lax.axis_size("c")
    core = lax.axis_index("c").astype(jnp.int32).reshape(1)
    every = pltpu.with_memory_space_constraint(every, pltpu.HBM)
    other = half_product(every, weight, 1 - core, n_tensor)
    other = lax.ppermute(other, "c", [(0, 1), (1, 0)])
    own = half_product(every, weight, core, n_tensor)
    share = (own.astype(jnp.float32) + other.astype(jnp.float32)).astype(jnp.bfloat16)
    shares = lax.all_to_all(share, ("x", "l"), split_axis=0, concat_axis=0, tiled=True)
    mixed = jnp.sum(
        shares.reshape(n_tensor // n_c, -1, col_width).astype(jnp.float32), axis=0
    ).astype(jnp.bfloat16)
    return (mixed, codes_t, scales_t)


def solution(mesh):
    fine = Mesh(mesh.devices.reshape(SIZES), AXES)
    return jax.shard_map(
        body,
        mesh=fine,
        in_specs=(P(FSDP + TENSOR, None), P(), P(FSDP, TENSOR), P(FSDP, TENSOR)),
        out_specs=(P(TENSOR, FSDP), P(FSDP, TENSOR), P(FSDP, TENSOR)),
        check_vma=False,
    )
```

```python
import functools

import jax
import jax.numpy as jnp
from jax import lax
from jax.experimental import pallas as pl
from jax.experimental.pallas import tpu as pltpu
from jax.sharding import Mesh, PartitionSpec as P

TILE = 128
EPSILON = 1e-06
AXES = ("z", "h", "x", "l", "c")
SIZES = (8, 4, 4, 2, 2)
FSDP = ("z", "h")
TENSOR = ("x", "l", "c")
PACK_STEPS = 1
GROUP = 4


def pack_kernel(in_ref, *refs):
    *out_refs, scratch = refs
    rows = in_ref.shape[0]
    sections, packed_rows, lanes = out_refs[0].shape
    tiles = packed_rows // rows
    for section in range(sections):
        for which, out_ref in enumerate(out_refs):
            for tile in range(tiles):
                at = ((section * len(out_refs) + which) * tiles + tile) * lanes
                scratch[which, pl.ds(tile * rows, rows), :] = in_ref[:, pl.ds(at, lanes)].astype(
                    jnp.float32
                )
            out_ref[section] = scratch[which].astype(jnp.bfloat16)


def pack(old_codes, n_fsdp, parts):
    rows, width = old_codes.shape
    packed_rows = rows * width // n_fsdp // TILE // parts
    sections = n_fsdp // PACK_STEPS
    shape = jax.ShapeDtypeStruct((n_fsdp, packed_rows, TILE), jnp.bfloat16)
    block = pl.BlockSpec((sections, packed_rows, TILE), lambda i: (i, 0, 0))
    return pl.pallas_call(
        pack_kernel,
        out_shape=(shape,) * parts,
        grid=(PACK_STEPS,),
        in_specs=[pl.BlockSpec((rows, width // PACK_STEPS), lambda i: (0, i))],
        out_specs=(block,) * parts,
        scratch_shapes=[pltpu.VMEM((parts, packed_rows, TILE), jnp.float32)],
        compiler_params=pltpu.CompilerParams(vmem_limit_bytes=16 << 20),
        name="pack",
    )(old_codes)


def requantize_kernel(scale_ref, in_ref, codes_ref, weight_ref, new_scale_ref, rows_ref, piece_ref):
    senders, parts, packed_rows, _ = in_ref.shape
    total_rows, width = rows_ref.shape
    tiles = width // TILE
    rows = packed_rows // tiles

    for part in range(parts):
        for sender in range(senders):
            slot = sender % 2
            piece_ref[slot] = in_ref[sender, part].astype(jnp.float32)
            base = (part * senders + sender) * rows
            for tile in range(tiles):
                rows_ref[pl.ds(base, rows), tile * TILE : (tile + 1) * TILE] = piece_ref[
                    slot, pl.ds(tile * rows, rows), :
                ]
    lane = lax.broadcasted_iota(jnp.int32, (1, TILE), 1)

    def one_row(row, carry):
        at = pl.ds(pl.multiple_of(row * TILE, TILE), TILE)
        line = jnp.zeros((1, TILE), jnp.float32)
        for tile in range(tiles):
            cols = slice(tile * TILE, (tile + 1) * TILE)
            codes = rows_ref[at, cols]
            scale = scale_ref[row, tile]
            top = jnp.max(jnp.abs(codes), axis=0, keepdims=True)
            new_scale = jnp.max(top, axis=1, keepdims=True) * scale + EPSILON
            line = jnp.where(lane == tile, new_scale, line)
            new_codes = (codes * scale / new_scale).astype(jnp.bfloat16)
            codes_ref[at, cols] = new_codes
            weight_ref[at, cols] = (new_codes.astype(jnp.float32) * new_scale).astype(jnp.bfloat16)
        new_scale_ref[pl.ds(row, 1), :] = line
        return carry

    lax.fori_loop(0, total_rows // TILE, one_row, 0)


def requantize(moved, scale_block, width):
    senders, parts, packed_rows, _ = moved.shape
    total_rows = senders * parts * packed_rows * TILE // width
    vmem = pl.BlockSpec(memory_space=pltpu.VMEM)
    return pl.pallas_call(
        requantize_kernel,
        out_shape=(
            jax.ShapeDtypeStruct((total_rows, width), jnp.bfloat16),
            jax.ShapeDtypeStruct((total_rows, width), jnp.bfloat16),
            jax.ShapeDtypeStruct((total_rows // TILE, TILE), jnp.float32),
        ),
        in_specs=[pl.BlockSpec(memory_space=pltpu.SMEM), vmem],
        out_specs=(vmem, vmem, vmem),
        scratch_shapes=[
            pltpu.VMEM((total_rows, width), jnp.float32),
            pltpu.VMEM((2, packed_rows, TILE), jnp.float32),
        ],
        compiler_params=pltpu.CompilerParams(vmem_limit_bytes=20 << 20),
        name="requantize",
    )(scale_block, moved)


def half_product_kernel(parity_ref, *refs):
    *token_refs, weight_ref, out_ref = refs
    tokens = jnp.concatenate([ref[...] for ref in token_refs], axis=0)
    out_ref[...] = jnp.dot(
        tokens, weight_ref[...], preferred_element_type=jnp.float32
    ).astype(jnp.bfloat16)


def owner_block(member, step, parity_ref):
    return 2 * (step * GROUP + member) + parity_ref[0], 0


def half_product(every, weight, parity, owners):
    depth, width = weight.shape
    rows = every.shape[0] // owners
    count = every.shape[0] // 2
    return pl.pallas_call(
        half_product_kernel,
        out_shape=jax.ShapeDtypeStruct((count, width), jnp.bfloat16),
        grid_spec=pltpu.PrefetchScalarGridSpec(
            num_scalar_prefetch=1,
            grid=(owners // (2 * GROUP),),
            in_specs=[
                pl.BlockSpec((rows, depth), functools.partial(owner_block, member))
                for member in range(GROUP)
            ]
            + [pl.BlockSpec(memory_space=pltpu.VMEM)],
            out_specs=pl.BlockSpec((GROUP * rows, width), lambda i, parity: (i, 0)),
        ),
        compiler_params=pltpu.CompilerParams(vmem_limit_bytes=14 << 20),
        cost_estimate=pl.CostEstimate(
            flops=2 * count * depth * width,
            bytes_accessed=2 * (count * depth + depth * width + count * width),
            transcendentals=0,
        ),
        name="half_product",
    )(parity, *(every,) * GROUP, weight)


def body(old_codes, old_scales, gate_pre, up_pre):
    n_fsdp = lax.axis_size(FSDP)
    n_tensor = lax.axis_size(TENSOR)
    f_index = lax.axis_index(FSDP)
    t_index = lax.axis_index(TENSOR)
    block_rows, full_width = old_codes.shape
    col_width = full_width // n_fsdp
    col_tiles = col_width // TILE
    per_owner = n_fsdp // n_tensor
    own_rows = block_rows * n_fsdp
    row_tiles = own_rows // TILE
    hidden = (jax.nn.silu(gate_pre.astype(jnp.float32)) * up_pre.astype(jnp.float32)).astype(
        jnp.bfloat16
    )
    n_z = lax.axis_size("z")
    n_h = lax.axis_size("h")
    near = lax.all_gather(hidden, "h", axis=0, tiled=True)
    staged, direct = pack(old_codes, n_fsdp, 2)
    part_rows = staged.shape[1]
    packed_rows = 2 * part_rows

    def swapped(sections, rows):
        return jnp.swapaxes(sections.reshape(rows, -1, part_rows, TILE), 0, 1).reshape(
            n_fsdp, part_rows, TILE
        )

    along_z = lax.all_to_all(staged, "z", split_axis=0, concat_axis=0, tiled=True)
    near, along_z = lax.optimization_barrier((near, along_z))
    every = lax.all_gather(near, "z", axis=0, tiled=True)
    staged = lax.all_to_all(swapped(along_z, n_z), "h", split_axis=0, concat_axis=0, tiled=True)
    staged, direct = lax.optimization_barrier((staged, direct))
    direct = lax.all_to_all(direct, FSDP, split_axis=0, concat_axis=0, tiled=True)
    sectioned = jnp.concatenate([swapped(staged, n_h), direct], axis=1)
    moved = lax.all_to_all(
        sectioned.reshape(n_tensor, per_owner * packed_rows, TILE),
        TENSOR,
        split_axis=0,
        concat_axis=0,
        tiled=True,
    )
    scale_block = lax.dynamic_slice(
        old_scales, (t_index * row_tiles, f_index * col_tiles), (row_tiles, col_tiles)
    )
    new_codes, weight, new_scale = requantize(
        moved.reshape(n_tensor, per_owner, packed_rows, TILE), scale_block, col_width
    )
    codes_t = new_codes.T
    scales_t = new_scale[:, :col_tiles].T

    n_c = lax.axis_size("c")
    core = lax.axis_index("c").astype(jnp.int32).reshape(1)
    every = pltpu.with_memory_space_constraint(every, pltpu.HBM)
    other = half_product(every, weight, 1 - core, n_tensor)
    other = lax.ppermute(other, "c", [(0, 1), (1, 0)])
    own = half_product(every, weight, core, n_tensor)
    share = (own.astype(jnp.float32) + other.astype(jnp.float32)).astype(jnp.bfloat16)
    shares = lax.all_to_all(share, ("x", "l"), split_axis=0, concat_axis=0, tiled=True)
    mixed = jnp.sum(
        shares.reshape(n_tensor // n_c, -1, col_width).astype(jnp.float32), axis=0
    ).astype(jnp.bfloat16)
    return (mixed, codes_t, scales_t)


def solution(mesh):
    fine = Mesh(mesh.devices.reshape(SIZES), AXES)
    return jax.shard_map(
        body,
        mesh=fine,
        in_specs=(P(FSDP + TENSOR, None), P(), P(FSDP, TENSOR), P(FSDP, TENSOR)),
        out_specs=(P(TENSOR, FSDP), P(FSDP, TENSOR), P(FSDP, TENSOR)),
        check_vma=False,
    )
```
